256 devices in a mesh: seq: 32 (over y, x, core), mp: 8 (over z).
Axes of the slice: x: 4, y: 4, z: 8, core: 2. Of those that a mesh axis runs over, the one named last changes fastest.
Arguments:
- projections: bfloat16 [3, 4096, 49152], P(None, 'mp', 'seq'), may hold values from -6 to 6
- lengths: int32 [128], replicated, may hold values from 1 to 1536, as said below
- owners: int32 [128], replicated, may hold values from 0 to 31, as said below
- offsets: int32 [128], replicated, may hold values from 0 to 32767, as said below
- short_filter: float32 [3, 256, 7], replicated, may hold values from -2 to 2
- long_filter: bfloat16 [256, 128], replicated, may hold values from -0.9 to 0.9
- skip: float32 [4096], replicated, may hold values from -4 to 4
- out_weight: bfloat16 [4096, 8192], P('seq', 'mp'), may hold values from -0.09375 to 0.09375
Outputs:
- mixed: bfloat16 [32768, 8192], P('seq', 'mp')
The draws below stay inside these ranges and needn't reach their ends.
Inputs may be any that keep to these rules, and one draw needn't show every extreme that they name: lengths[r] is the number of tokens of request r in packing order; the lengths sum to 32768. In every draw one request is 1536 tokens long and the last request is one token long. owners never decrease along r and name every index of seq; owner o keeps its requests, in packing order, in the first rows of its block of 1536 rows of projections, and the rows after them are unused. offsets[r] is the sum of the lengths before r. The first request of owner o starts within 256 of o * 1024; in every draw some owner starts exactly 256 before that mark and the next owner exactly 256 after its own, so that owner's requests fill all 1536 rows of its block; the last owner starts exactly 256 after its mark.
All inputs are finite; a program needn't handle non-finite values.
Results may differ from the reference program's by a relative error of at most 0.0064.
Values may be sent and summed in bfloat16 or wider, within the bound.
A program may use at most 128 MiB of HBM per device.

```python
import jax
import jax.numpy as jnp
from jax import lax

DOUT = 8192
CH = 4096
GSIZE = 16
SHORT = 7
LONG = 128
TOK_DEV = 1024
SPILL = 256
CAP = 1536
TOKENS = 32768
GROUPS = 256
REQS = 128
N_SEQ = 32


def packing_layout(key):
    base_key = jax.random.fold_in(key, 7)
    drift_key, marked_key, shuffle_key = jax.random.split(base_key, 3)
    total_tokens = TOK_DEV * N_SEQ
    drift = jax.random.randint(drift_key, (N_SEQ + 1,), -SPILL, SPILL + 1)
    chosen = jax.random.randint(marked_key, (), 1, N_SEQ - 1)
    owner_ids = jnp.arange(N_SEQ + 1, dtype=jnp.int32)
    drift = jnp.where(owner_ids == chosen, -SPILL, drift)
    drift = jnp.where(owner_ids == chosen + 1, SPILL, drift)
    drift = jnp.where(owner_ids == N_SEQ - 1, SPILL, drift)
    drift = jnp.where((owner_ids == 0) | (owner_ids == N_SEQ), 0, drift)
    bounds = (owner_ids * TOK_DEV + drift).astype(jnp.int32)
    inner_bounds = bounds[1:N_SEQ]
    chosen_begin = jnp.sum(jnp.where(owner_ids == chosen, bounds, 0))
    chosen_end = jnp.sum(jnp.where(owner_ids == chosen + 1, bounds, 0))
    shuffled = (jax.random.permutation(shuffle_key, total_tokens - 1) + 1).astype(jnp.int32)
    hit_bound = jnp.any(shuffled[:, None] == inner_bounds[None, :], axis=1)
    inside = (shuffled > chosen_begin) & (shuffled < chosen_end)
    last_cut = shuffled == total_tokens - 1
    taken = (hit_bound | inside | last_cut).astype(jnp.int32)
    ordering = jnp.argsort(taken, stable=True)
    extra_cuts = shuffled[ordering[:REQS - N_SEQ - 1]]
    forced = jnp.full((1,), total_tokens - 1, jnp.int32)
    request_starts = jnp.sort(jnp.concatenate([bounds[:N_SEQ], extra_cuts, forced])).astype(jnp.int32)
    request_ends = jnp.concatenate([request_starts[1:], jnp.full((1,), total_tokens, jnp.int32)])
    request_lengths = (request_ends - request_starts).astype(jnp.int32)
    request_owner = jnp.sum((request_starts[:, None] >= inner_bounds[None, :]).astype(jnp.int32), axis=1).astype(jnp.int32)
    return (request_lengths, request_owner, request_starts)


def draw_lengths(key, part):
    return packing_layout(key)[0]


def draw_owners(key, part):
    return packing_layout(key)[1]


def draw_offsets(key, part):
    return packing_layout(key)[2]


def draw_long_filter(key, part):
    tap_key, rate_key = jax.random.split(jax.random.fold_in(key, 3))
    unit = jax.random.uniform(rate_key, (GROUPS, 1), jnp.float32)
    lag_values = jnp.arange(LONG, dtype=jnp.float32)[None, :]
    taps = jnp.clip(jax.random.normal(tap_key, (GROUPS, LONG), jnp.float32), -6.0, 6.0)
    rate = jnp.exp(jnp.log(1.0 / 400.0) + unit * (jnp.log(1.0 / 12.0) - jnp.log(1.0 / 400.0)))
    return (0.15 * taps * jnp.exp(-rate * lag_values)).astype(jnp.bfloat16)


def block_levels(key, extent, shards, low, top_value):
    loudness = 1.0
    for dim, shards_of in shards:
        heights = jax.random.uniform(jax.random.fold_in(jax.random.fold_in(key, 6), dim), (shards_of,), jnp.float32, low / len(shards), top_value / len(shards))
        loudness = loudness * jnp.repeat(jnp.exp(heights), extent[dim] // shards_of).reshape((-1,) + (1,) * (len(extent) - 1 - dim))
    return loudness


def bell_draw(stream_key, shape, deviation, limit, pieces=(), held_as=jnp.bfloat16):
    drawn = jax.random.normal(stream_key, shape, jnp.float32) * deviation
    if len(pieces) > 0:
        drawn = block_levels(stream_key, shape, pieces, -0.22, 0.18) * drawn
    return jnp.clip(drawn, min=-limit, max=limit).astype(held_as)


def setup_inputs(seed: int = 0) -> dict:
    key_of = jax.random.split(jax.random.key(seed), 9)
    projections = bell_draw(key_of[0], (3, CH, N_SEQ * CAP), 1.0, 6.0, ((1, 8), (2, 32)))
    lengths = draw_lengths(jax.random.fold_in(key_of[8], 71), 0)
    owners = draw_owners(jax.random.fold_in(key_of[8], 71), 0)
    offsets = draw_offsets(jax.random.fold_in(key_of[8], 71), 0)
    short_filter = bell_draw(key_of[4], (3, GROUPS, SHORT), SHORT ** -0.5, 2.0, (), jnp.float32)
    long_filter = draw_long_filter(jax.random.fold_in(key_of[8], 71), 0)
    skip = bell_draw(key_of[6], (CH,), 1.0, 4.0, (), jnp.float32)
    out_weight = bell_draw(key_of[7], (CH, DOUT), CH ** -0.5, 0.09375, ((0, 32), (1, 8)))
    return {"projections": projections, "lengths": lengths, "owners": owners, "offsets": offsets, "short_filter": short_filter, "long_filter": long_filter, "skip": skip, "out_weight": out_weight}


def running_mark(offsets, marks, total):
    marked = jnp.zeros((total,), jnp.int32).at[offsets].max(marks)
    return lax.cummax(marked, axis=0)


def masked_long(product, taps, position):
    width, length = product.shape
    blocks = length // LONG
    current = product.reshape(width, blocks, LONG)
    earlier = jnp.concatenate([jnp.zeros((width, 1, LONG), product.dtype), current[:, :-1]], axis=1)
    window = jnp.concatenate([earlier, current], axis=2)
    inner = jnp.arange(2 * LONG, dtype=jnp.int32)[:, None]
    outer = jnp.arange(LONG, dtype=jnp.int32)[None, :]
    lag_table = outer + LONG - inner
    valid = (lag_table >= 0) & (lag_table < LONG)
    kernel = jnp.where(valid, taps[jnp.clip(lag_table, 0, LONG - 1)], jnp.zeros((), product.dtype))
    allowed = lag_table[None] <= position.reshape(blocks, 1, LONG)
    matrix = jnp.where(allowed, kernel[None], jnp.zeros((), product.dtype))
    return jnp.einsum("kbi,bio->kbo", window, matrix).reshape(width, length)


def reference(projections, lengths, owners, offsets, short_filter, long_filter, skip, out_weight):
    token_ids = jnp.arange(TOKENS, dtype=jnp.int32)
    request_of = running_mark(offsets, jnp.arange(REQS, dtype=jnp.int32), TOKENS)
    length_begins = (jnp.cumsum(lengths) - lengths).astype(jnp.int32)
    request_begin = running_mark(length_begins, length_begins, TOKENS)
    position = token_ids - request_begin
    member = owners[None, :] == jnp.arange(N_SEQ, dtype=jnp.int32)[:, None]
    owner_first = jnp.min(jnp.where(member, offsets[None, :], TOKENS), axis=1)
    owner_at = owners[request_of]
    source = owner_at * CAP + token_ids - owner_first[owner_at]

    def one_group(group):
        panels = lax.dynamic_slice_in_dim(projections, group * GSIZE, GSIZE, 1)
        packed = jnp.take(panels, source, axis=2).astype(jnp.float32)
        padded = jnp.pad(packed, ((0, 0), (0, 0), (SHORT - 1, 0)))
        short_taps = lax.dynamic_index_in_dim(short_filter, group, 1, keepdims=False).astype(jnp.float32)
        summed = jnp.zeros(packed.shape, packed.dtype)
        for lag_step in range(SHORT):
            window = padded[:, :, SHORT - 1 - lag_step:SHORT - 1 - lag_step + TOKENS]
            summed = summed + jnp.where(lag_step <= position, short_taps[:, lag_step][:, None, None] * window, jnp.zeros((), packed.dtype))
        query = summed[0].astype(jnp.bfloat16)
        product = (summed[1] * summed[2]).astype(jnp.bfloat16)
        query, product = lax.optimization_barrier((query, product))
        product_wide = product.astype(jnp.float32)
        long_taps = lax.dynamic_index_in_dim(long_filter, group, 0, keepdims=False).astype(jnp.float32)
        gains = lax.dynamic_slice_in_dim(skip, group * GSIZE, GSIZE, 0)
        value = masked_long(product_wide, long_taps, position) + gains[:, None] * product_wide
        return (query.astype(jnp.float32) * value).astype(jnp.bfloat16)

    gated = lax.map(one_group, jnp.arange(GROUPS, dtype=jnp.int32)).reshape(CH, TOKENS)
    return jnp.dot(gated.T, out_weight, preferred_element_type=jnp.float32).astype(jnp.bfloat16)
```

```python
import functools

import jax
import jax.numpy as jnp
from jax import lax
from jax.experimental import pallas as pl
from jax.experimental.pallas import tpu as pltpu
from jax.sharding import PartitionSpec as P

MESH = pl.DeviceIdType.MESH
F32 = jnp.float32
BF16 = jnp.bfloat16

GSIZE = 16
SHORT = 7
LONG = 128
TOK = 1024
SPILL = 256
CAP = 1536
TOKENS = 32768
WIDE = 128
CHUNKS = 4
GROUPS = WIDE // GSIZE
BLOCKS = CAP // LONG
REACH = 2 * SPILL


def iota(shape, dim):
    return lax.broadcasted_iota(jnp.int32, shape, dim)


def prepare(seq, model, offsets, owners, long_filter, masks, later, taps, pick, product, gated):
    off = offsets[...]
    own = owners[...]
    first = jnp.min(jnp.where(own == seq, off, TOKENS), axis=1, keepdims=True)
    after = jnp.min(jnp.where(own == seq + 1, off, TOKENS), axis=1, keepdims=True)
    column = jnp.broadcast_to(off, (LONG, LONG)).T
    inner = iota((LONG, LONG), 0)
    outer = iota((LONG, LONG), 1)
    lag = outer - inner
    for b in range(BLOCKS):
        token = first + iota((1, LONG), 1) + b * LONG
        begin = jnp.max(jnp.where(column <= token, column, 0), axis=0, keepdims=True)
        pos = token - begin
        older = (lag < 0) & (lag + LONG <= pos)
        newer = (lag >= 0) & (lag <= pos)
        masks[b, 0:LONG, :] = jnp.where(older, 1.0, 0.0).astype(BF16)
        masks[b, LONG : 2 * LONG, :] = jnp.where(newer, 1.0, 0.0).astype(BF16)
        later[:, b * LONG : (b + 1) * LONG] = jnp.broadcast_to(
            jnp.where(pos >= 1, 1.0, 0.0), (8, LONG)
        )
    rows = CHUNKS * GROUPS
    taps[...] = long_filter[pl.ds(pl.multiple_of(model * rows, rows), rows), :].astype(F32)
    shift = first - seq * TOK + SPILL
    turned = iota((SPILL, 3 * SPILL), 1) - iota((SPILL, 3 * SPILL), 0) - REACH
    pick[...] = jnp.where(turned == -shift, 1.0, 0.0).astype(BF16)
    product[:, 0:LONG] = jnp.zeros((WIDE, LONG), BF16)
    gated[:, 0:REACH] = jnp.zeros((WIDE, REACH), BF16)
    return after - first + shift


def filter_chunk(model, chunk, panels, short_filter, skip, masks, later, taps, circ, direct, query, product, gated):
    row = model * CHUNKS * GROUPS + chunk * GROUPS
    gains = skip[pl.ds(model * CHUNKS + chunk, 1), :]
    direct[...] = jnp.broadcast_to(gains, (WIDE, WIDE)).T
    mask1 = jnp.concatenate([later[...], later[...]], axis=0)

    def short(g, _):
        ch = pl.ds(pl.multiple_of(g * GSIZE, GSIZE), GSIZE)
        line = jnp.broadcast_to(taps[pl.ds(chunk * GROUPS + g, 1), :], (LONG, LONG))
        circ[g] = pltpu.roll(line, 0, 1, stride=1, stride_axis=0).astype(BF16)
        sums = []
        for p in range(3):
            x = panels[p, ch, :].astype(F32)
            f = short_filter[p, pl.ds(row + g, 1), :]
            y = f[:, SHORT - 1 : SHORT] * x
            for j in range(SHORT - 2, -1, -1):
                y = f[:, j : j + 1] * x + mask1 * pltpu.roll(y, 1, 1)
            sums.append(y)
        query[ch, :] = sums[0].astype(BF16)
        product[ch, LONG:] = (sums[1] * sums[2]).astype(BF16)
        return 0

    lax.fori_loop(0, GROUPS, short, 0)

    def long(b, _):
        at = pl.multiple_of(b * LONG, LONG)
        older = masks[b, 0:LONG, :]
        newer = masks[b, LONG : 2 * LONG, :]
        for g in range(GROUPS):
            ch = slice(g * GSIZE, (g + 1) * GSIZE)
            matrix = jnp.concatenate([circ[g] * older, circ[g] * newer], axis=0)
            window = product[ch, pl.ds(at, 2 * LONG)]
            w = jnp.dot(window, matrix, preferred_element_type=F32)
            now = product[ch, pl.ds(at + LONG, LONG)].astype(F32)
            w = w + direct[ch, :] * now
            out = query[ch, pl.ds(at, LONG)].astype(F32) * w
            gated[ch, pl.ds(at + REACH, LONG)] = out.astype(BF16)
        return 0

    lax.fori_loop(0, BLOCKS, long, 0)


def place(limit, k, pick, gated):
    at = k * SPILL
    if not isinstance(k, int):
        at = pl.multiple_of(at, SPILL)
    block = gated[:, pl.ds(at, 3 * SPILL)]
    moved = lax.dot_general(
        pick[...], block, (((1,), (1,)), ((), ())), preferred_element_type=F32
    )
    mine = iota((SPILL, WIDE), 0) + k * SPILL < limit
    return jnp.where(mine, moved, 0.0).astype(BF16)


def filter_kernel(panels, offsets, owners, short_filter, long_filter, skip, out, masks, later, taps, pick, limit, circ, direct, query, product, gated):
    seq = lax.axis_index("seq")
    model = lax.axis_index("mp")
    chunk = pl.program_id(0)

    @pl.when(chunk == 0)
    def _():
        end = prepare(seq, model, offsets, owners, long_filter, masks, later, taps, pick, product, gated)
        limit[...] = jnp.broadcast_to(end, limit.shape)

    filter_chunk(model, chunk, panels, short_filter, skip, masks, later, taps, circ, direct, query, product, gated)
    for k in range(CAP // SPILL):
        out[0, k * SPILL : (k + 1) * SPILL, :] = place(limit[0:1, 0:1], k, pick, gated)


def filter_call(projections, offsets, owners, short_filter, long_filter, skip):
    whole = lambda shape: pl.BlockSpec(shape, lambda i: (0,) * len(shape))
    return pl.pallas_call(
        filter_kernel,
        grid=(CHUNKS,),
        out_shape=jax.ShapeDtypeStruct((CHUNKS, CAP, WIDE), BF16),
        in_specs=[
            pl.BlockSpec((3, WIDE, CAP), lambda i: (0, i, 0)),
            whole(offsets.shape),
            whole(owners.shape),
            whole(short_filter.shape),
            whole(long_filter.shape),
            whole(skip.shape),
        ],
        out_specs=pl.BlockSpec((1, CAP, WIDE), lambda i: (i, 0, 0)),
        scratch_shapes=[
            pltpu.VMEM((BLOCKS, 2 * LONG, LONG), BF16),
            pltpu.VMEM((8, CAP), F32),
            pltpu.VMEM((CHUNKS * GROUPS, LONG), F32),
            pltpu.VMEM((SPILL, 3 * SPILL), BF16),
            pltpu.VMEM((8, 128), jnp.int32),
            pltpu.VMEM((GROUPS, LONG, LONG), BF16),
            pltpu.VMEM((WIDE, WIDE), F32),
            pltpu.VMEM((WIDE, CAP), BF16),
            pltpu.VMEM((WIDE, LONG + CAP), BF16),
            pltpu.VMEM((WIDE, REACH + CAP), BF16),
        ],
    )(projections, offsets, owners, short_filter, long_filter, skip)


N_MP = 8
SIDE = 4
DEPTH = 4 * WIDE
COLS = 1024
ROWS_W = WIDE
HALF = TOK // 2
PIECES = 2 * CHUNKS


def position():
    seq = lax.axis_index("seq")
    return seq, lax.axis_index("mp"), seq // 8, (seq // 2) % SIDE, seq % 2


def seq_at(y, x, core):
    return ((y % SIDE) * SIDE + x % SIDE) * 2 + core


class Links:
    def __init__(self, held, weight, left, right, sems):
        self.held, self.weight, self.left, self.right = held, weight, left, right
        (self.zs, self.zr, self.xs, self.xr, self.ys, self.yr, self.cs, self.cr, self.ss, self.sr) = sems
        self.seq, self.mp, self.y, self.x, self.core = position()

    def enter(self):
        barrier = pltpu.get_barrier_semaphore()
        targets = [{"mp": (self.mp + d) % N_MP} for d in (1, N_MP - 1)]
        targets += [{"seq": (self.seq + d) % 32} for d in (1, 31)]
        targets += [{"seq": seq_at(self.y, self.x + d, self.core)} for d in (1, SIDE - 1)]
        targets += [{"seq": seq_at(self.y + d, self.x, self.core)} for d in (1, SIDE - 1)]
        targets += [{"seq": seq_at(self.y, self.x, 1 - self.core)}]
        for target in targets:
            pl.semaphore_signal(barrier, inc=1, device_id=target, device_id_type=MESH)
        pl.semaphore_wait(barrier, len(targets))

    def z_copy(self, way, step, piece):
        src = (self.mp + (N_MP - step if way == 0 else step)) % N_MP
        ref = self.held.at[src, piece % 2, piece // 2]
        to = (self.mp + (1 if way == 0 else N_MP - 1)) % N_MP
        return pltpu.make_async_remote_copy(
            ref, ref, self.zs.at[way, step, piece], self.zr.at[way, step, piece],
            device_id={"mp": to}, device_id_type=MESH,
        )

    def z_arrived(self, way, step, piece):
        src = (self.mp + (N_MP - step - 1 if way == 0 else step + 1)) % N_MP
        ref = self.held.at[src, piece % 2, piece // 2]
        pltpu.make_async_remote_copy(
            ref, ref, self.zs.at[way, step, piece], self.zr.at[way, step, piece],
            device_id={"mp": self.mp}, device_id_type=MESH,
        ).wait_recv()

    def w_rows(self, y, x, part):
        at = seq_at(y, x, self.core) * ROWS_W
        size = ROWS_W
        if part is not None:
            size = ROWS_W // 2
            at = at + part * size
        return self.weight.at[pl.ds(pl.multiple_of(at, size), size), :]

    def w_copy(self, send, recv, ref, to):
        return pltpu.make_async_remote_copy(
            ref, ref, send, recv, device_id={"seq": to}, device_id_type=MESH
        )

    def x_copy(self, way, step):
        d = 1 if way == 0 else SIDE - 1
        ref = self.w_rows(self.y, self.x + step * (SIDE - d), None if step == 0 else way)
        return self.w_copy(self.xs.at[way, step], self.xr.at[way, step], ref, seq_at(self.y, self.x + d, self.core))

    def x_arrived(self, way, step):
        d = 1 if way == 0 else SIDE - 1
        ref = self.w_rows(self.y, self.x + (step + 1) * (SIDE - d), None if step == 0 else way)
        self.w_copy(self.xs.at[way, step], self.xr.at[way, step], ref, self.seq).wait_recv()

    def y_copy(self, way, step, dx):
        d = 1 if way == 0 else SIDE - 1
        ref = self.w_rows(self.y + step * (SIDE - d), self.x + dx, None if step == 0 else way)
        return self.w_copy(
            self.ys.at[way, step, dx], self.yr.at[way, step, dx], ref, seq_at(self.y + d, self.x, self.core)
        )

    def y_arrived(self, way, step, dx):
        d = 1 if way == 0 else SIDE - 1
        ref = self.w_rows(self.y + (step + 1) * (SIDE - d), self.x + dx, None if step == 0 else way)
        self.w_copy(self.ys.at[way, step, dx], self.yr.at[way, step, dx], ref, self.seq).wait_recv()

    def c_copy(self, dy, dx):
        ref = self.w_rows(self.y + dy, self.x + dx, None)
        return self.w_copy(
            self.cs.at[dy, dx], self.cr.at[dy, dx], ref, seq_at(self.y, self.x, 1 - self.core)
        )

    def c_arrived(self, dy, dx):
        at = seq_at(self.y + dy, self.x + dx, 1 - self.core) * ROWS_W
        ref = self.weight.at[pl.ds(pl.multiple_of(at, ROWS_W), ROWS_W), :]
        self.w_copy(self.cs.at[dy, dx], self.cr.at[dy, dx], ref, self.seq).wait_recv()

    def s_copy(self, way, chunk, ref):
        into = (self.left if way == 0 else self.right).at[chunk]
        to = (self.seq + (1 if way == 0 else 31)) % 32
        return pltpu.make_async_remote_copy(
            ref, into, self.ss.at[way, chunk], self.sr.at[way, chunk],
            device_id={"seq": to}, device_id_type=MESH,
        )

    def w_begin(self):
        for way in (0, 1):
            self.x_copy(way, 0).start()
            self.y_copy(way, 0, 0).start()
        self.c_copy(0, 0).start()

    def w_row(self):
        for way, dx in ((0, SIDE - 1), (1, 1)):
            self.x_arrived(way, 0)
            self.x_copy(way, 1).start()
            for to in (0, 1):
                self.y_copy(to, 0, dx).start()
            self.c_copy(0, dx).start()

    def w_far(self):
        for way in (0, 1):
            self.x_arrived(way, 1)
        for to in (0, 1):
            self.y_copy(to, 0, 2).start()
        self.c_copy(0, 2).start()

    def w_near(self, dx):
        for way, dy in ((0, SIDE - 1), (1, 1)):
            self.y_arrived(way, 0, dx)
            self.y_copy(way, 1, dx).start()
            self.c_copy(dy, dx).start()

    def w_last(self, dx):
        for way in (0, 1):
            self.y_arrived(way, 1, dx)
        self.c_copy(2, dx).start()

    def w_end(self):
        for dy in range(SIDE):
            for dx in range(SIDE):
                self.c_arrived(dy, dx)

    def relay(self, step, piece0, piece1):
        self.z_arrived(0, step - 1, piece0)
        self.z_copy(0, step, piece0).start()
        self.z_arrived(1, step - 1, piece1)
        self.z_copy(1, step, piece1).start()

    def leave(self):
        for way in (0, 1):
            for step in range(2):
                self.x_copy(way, step).wait_send()
                for dx in range(SIDE):
                    self.y_copy(way, step, dx).wait_send()

            def drain(n, _):
                self.z_copy(way, n // PIECES, n % PIECES).wait_send()
                return 0

            lax.fori_loop(0, 3 * PIECES, drain, 0)
            for piece in range(CHUNKS):
                self.z_copy(way, 3, piece + way * CHUNKS).wait_send()
        for dy in range(SIDE):
            for dx in range(SIDE):
                self.c_copy(dy, dx).wait_send()


COLS_STEP = 256


def part_product(held, weight, src, half, chunks, cols):
    lhs = jnp.concatenate([held[src, half, q] for q in chunks], axis=1)
    rhs = jnp.concatenate(
        [weight[pl.ds(pl.multiple_of((src * CHUNKS + q) * WIDE, WIDE), WIDE), cols] for q in chunks], axis=0
    )
    return jnp.dot(lhs, rhs, preferred_element_type=F32)


def columns(n):
    return pl.ds(pl.multiple_of(n * COLS_STEP, COLS_STEP), COLS_STEP)


def add_product(held, weight, total, src, half, chunks):
    def body(n, _):
        cols = columns(n)
        total[half, :, cols] += part_product(held, weight, src, half, chunks, cols)
        return 0

    lax.fori_loop(0, COLS // COLS_STEP, body, 0)


def finish(held, weight, total, staged, src, half, chunks):
    def body(n, _):
        cols = columns(n)
        value = total[half, :, cols] + part_product(held, weight, src, half, chunks, cols)
        staged[half, :, cols] = value.astype(BF16)
        return 0

    lax.fori_loop(0, COLS // COLS_STEP, body, 0)


def source_of(mp, u):
    p = u // 2
    far = (p + 1) // 2
    return (mp + N_MP + far * (1 - 2 * (p % 2))) % N_MP


def add_sources(held, weight, total, mp, low, high):
    def body(u, _):
        add_product(held, weight, total, source_of(mp, u), u % 2, range(CHUNKS))
        return 0

    lax.fori_loop(low, high, body, 0)


def mix_kernel(rows, own_weight, out, held, weight, total, staged, left, right, own_sem, out_sem, *sems):
    links = Links(held, weight, left, right, sems)
    mp = links.mp
    mine = pltpu.make_async_copy(own_weight, links.w_rows(links.y, links.x, None), own_sem)
    mine.start()
    links.enter()
    mine.wait()
    links.w_begin()
    for q in range(CHUNKS):
        links.s_copy(0, q, rows.at[q, CAP - SPILL : CAP]).start()
        links.s_copy(1, q, rows.at[q, 0:SPILL]).start()
    for q in range(CHUNKS):
        held[mp, 0, q] = rows[q, 2 * SPILL : 4 * SPILL]
        for way in (0, 1):
            links.z_copy(way, 0, 2 * q).start()
        for way in (0, 1):
            links.s_copy(way, q, rows.at[q, 0:SPILL]).wait_recv()
        held[mp, 1, q, 0:SPILL] = rows[q, SPILL : 2 * SPILL] + left[q]
        held[mp, 1, q, SPILL : 2 * SPILL] = rows[q, 4 * SPILL : 5 * SPILL] + right[q]
        for way in (0, 1):
            links.z_copy(way, 0, 2 * q + 1).start()
    total[...] = jnp.zeros_like(total)
    links.w_row()
    links.w_far()
    for k in range(PIECES):
        links.relay(1, k, k)
        if k < SIDE:
            links.w_near((0, SIDE - 1, 1, 2)[k])
    for k in range(PIECES):
        links.relay(2, k, k)
        if k < SIDE:
            links.w_last((0, SIDE - 1, 1, 2)[k])
        if k == SIDE:
            links.w_end()
    add_sources(held, weight, total, mp, 0, 6)
    for k in range(CHUNKS):
        links.relay(3, k, k + CHUNKS)
    add_sources(held, weight, total, mp, 6, 10)
    for k in range(CHUNKS):
        links.z_arrived(0, 2, k + CHUNKS)
        links.z_arrived(1, 2, k)
    add_sources(held, weight, total, mp, 10, 14)
    far = (mp + N_MP // 2) % N_MP
    for half in (0, 1):
        links.z_arrived(0, 3, half)
        links.z_arrived(1, 3, half + CHUNKS)
        add_product(held, weight, total, far, half, (0, 2))
    writes = []
    for half in (0, 1):
        links.z_arrived(0, 3, 2 + half)
        links.z_arrived(1, 3, 2 + half + CHUNKS)
        finish(held, weight, total, staged, far, half, (1, 3))
        if half == 0:
            spans = ((0, HALF, SPILL),)
        else:
            spans = ((0, SPILL, 0), (SPILL, HALF, TOK - SPILL))
        for n, (low, high, at) in enumerate(spans):
            copy = pltpu.make_async_copy(
                staged.at[half, low:high], out.at[at : at + high - low], out_sem.at[half, n]
            )
            copy.start()
            writes.append(copy)
    for q in range(CHUNKS):
        links.s_copy(0, q, rows.at[q, CAP - SPILL : CAP]).wait_send()
        links.s_copy(1, q, rows.at[q, 0:SPILL]).wait_send()
    links.leave()
    for copy in writes:
        copy.wait()


LINK_SCRATCH = [
    pltpu.VMEM((N_MP, 2, CHUNKS, HALF, WIDE), BF16),
    pltpu.VMEM((N_MP * DEPTH, COLS), BF16),
    pltpu.VMEM((2, HALF, COLS), F32),
    pltpu.VMEM((2, HALF, COLS), BF16),
    pltpu.VMEM((CHUNKS, SPILL, WIDE), BF16),
    pltpu.VMEM((CHUNKS, SPILL, WIDE), BF16),
    pltpu.SemaphoreType.DMA,
    pltpu.SemaphoreType.DMA((2, 2)),
    pltpu.SemaphoreType.DMA((2, 4, PIECES)),
    pltpu.SemaphoreType.DMA((2, 4, PIECES)),
    pltpu.SemaphoreType.DMA((2, 2)),
    pltpu.SemaphoreType.DMA((2, 2)),
    pltpu.SemaphoreType.DMA((2, 2, SIDE)),
    pltpu.SemaphoreType.DMA((2, 2, SIDE)),
    pltpu.SemaphoreType.DMA((SIDE, SIDE)),
    pltpu.SemaphoreType.DMA((SIDE, SIDE)),
    pltpu.SemaphoreType.DMA((2, CHUNKS)),
    pltpu.SemaphoreType.DMA((2, CHUNKS)),
]


def mix_call(rows, out_weight):
    vmem = pl.BlockSpec(memory_space=pltpu.VMEM)
    anywhere = pl.BlockSpec(memory_space=pl.ANY)
    return pl.pallas_call(
        mix_kernel,
        out_shape=jax.ShapeDtypeStruct((TOK, COLS), BF16),
        in_specs=[vmem, anywhere],
        out_specs=anywhere,
        scratch_shapes=LINK_SCRATCH,
        compiler_params=pltpu.CompilerParams(
            collective_id=0, has_side_effects=True, vmem_limit_bytes=60 * 2**20
        ),
    )(rows, out_weight)


def per_device(projections, lengths, owners, offsets, short_filter, long_filter, skip, out_weight):
    rows = filter_call(
        projections,
        offsets.reshape(1, -1),
        owners.reshape(1, -1),
        short_filter,
        long_filter,
        skip.reshape(-1, WIDE),
    )
    return mix_call(rows, out_weight)


def solution(mesh):
    placed = (P(None, "mp", "seq"), P(), P(), P(), P(), P(), P(), P("seq", "mp"))
    return jax.shard_map(
        per_device, mesh=mesh, in_specs=placed, out_specs=P("seq", "mp"), check_vma=False
    )
```

```python
import functools

import jax
import jax.numpy as jnp
from jax import lax
from jax.experimental import pallas as pl
from jax.experimental.pallas import tpu as pltpu
from jax.sharding import PartitionSpec as P

MESH = pl.DeviceIdType.MESH
F32 = jnp.float32
BF16 = jnp.bfloat16

GSIZE = 16
SHORT = 7
LONG = 128
TOK = 1024
SPILL = 256
CAP = 1536
TOKENS = 32768
WIDE = 128
CHUNKS = 4
GROUPS = WIDE // GSIZE
BLOCKS = CAP // LONG
REACH = 2 * SPILL


def iota(shape, dim):
    return lax.broadcasted_iota(jnp.int32, shape, dim)


def prepare(seq, model, offsets, owners, short_filter, long_filter, masks, later, near, taps, pick, product, gated):
    off = offsets[...]
    own = owners[...]
    first = jnp.min(jnp.where(own == seq, off, TOKENS), axis=1, keepdims=True)
    after = jnp.min(jnp.where(own == seq + 1, off, TOKENS), axis=1, keepdims=True)
    column = jnp.broadcast_to(off, (LONG, LONG)).T
    inner = iota((LONG, LONG), 0)
    outer = iota((LONG, LONG), 1)
    lag = outer - inner
    for b in range(BLOCKS):
        token = first + iota((1, LONG), 1) + b * LONG
        begin = jnp.max(jnp.where(column <= token, column, 0), axis=0, keepdims=True)
        pos = token - begin
        older = (lag < 0) & (lag + LONG <= pos)
        newer = (lag >= 0) & (lag <= pos)
        masks[b, 0:LONG, :] = jnp.where(older, 1.0, 0.0).astype(BF16)
        masks[b, LONG : 2 * LONG, :] = jnp.where(newer, 1.0, 0.0).astype(BF16)
        for j in range(1, SHORT):
            later[j - 1, :, b * LONG : (b + 1) * LONG] = jnp.broadcast_to(
                jnp.where(pos >= j, 1.0, 0.0), (8, LONG)
            )
    rows = CHUNKS * GROUPS
    taps[...] = long_filter[pl.ds(pl.multiple_of(model * rows, rows), rows), :].astype(F32)
    aside = pl.ds(pl.multiple_of(model // 4 * WIDE, WIDE), WIDE)
    for p in range(3):
        block = jnp.concatenate([short_filter[p, :, aside], jnp.zeros((WIDE - SHORT, WIDE), F32)], axis=0)
        near[p] = block.T
    shift = first - seq * TOK + SPILL
    turned = iota((SPILL, 3 * SPILL), 1) - iota((SPILL, 3 * SPILL), 0) - REACH
    pick[...] = jnp.where(turned == -shift, 1.0, 0.0).astype(BF16)
    product[:, 0:LONG] = jnp.zeros((WIDE, LONG), BF16)
    gated[:, 0:REACH] = jnp.zeros((WIDE, REACH), BF16)
    return after - first + shift


def short_stage(model, chunk, panels, near, skip, later, taps, circ, direct, query, product):
    row = model % 4 * (CHUNKS * GROUPS) + chunk * GROUPS
    gains = skip[pl.ds(model * CHUNKS + chunk, 1), :]
    direct[...] = jnp.broadcast_to(gains, (WIDE, WIDE)).T
    lane = iota((GSIZE, LONG), 1)

    def short(g, _):
        ch = pl.ds(pl.multiple_of(g * GSIZE, GSIZE), GSIZE)
        line = jnp.broadcast_to(taps[pl.ds(chunk * GROUPS + g, 1), :], (LONG, LONG))
        circ[g] = pltpu.roll(line, 0, 1, stride=1, stride_axis=0).astype(BF16)
        factor = []
        for p in range(3):
            f = near[p, pl.ds(row + g, 1), :]
            factor.append([jnp.broadcast_to(f[:, j : j + 1], (8, LONG)) for j in range(SHORT)])
        rolled = [[None] * SHORT for _ in range(3)]
        for b in range(BLOCKS):
            at = slice(b * LONG, (b + 1) * LONG)
            sums = []
            for p in range(3):
                x = panels[chunk, p, ch, at]
                wide = x.astype(F32)
                low = factor[p][0] * wide[0:8]
                high = factor[p][0] * wide[8:16]
                for j in range(1, SHORT):
                    turned = pltpu.roll(x, j, 1)
                    before = rolled[p][j]
                    rolled[p][j] = turned
                    if b > 0:
                        turned = jnp.where(lane < j, before, turned)
                    weight = factor[p][j] * later[j - 1, :, at]
                    wide = turned.astype(F32)
                    low = low + weight * wide[0:8]
                    high = high + weight * wide[8:16]
                sums.append(jnp.concatenate([low, high], axis=0))
            query[ch, at] = sums[0].astype(BF16)
            product[ch, (b + 1) * LONG : (b + 2) * LONG] = (sums[1] * sums[2]).astype(BF16)
        return 0

    lax.fori_loop(0, GROUPS, short, 0)


def long_stage(masks, circ, direct, query, product, gated):
    def long(b, _):
        at = pl.multiple_of(b * LONG, LONG)
        older = masks[b, 0:LONG, :]
        newer = masks[b, LONG : 2 * LONG, :]
        for g in range(GROUPS):
            ch = slice(g * GSIZE, (g + 1) * GSIZE)
            matrix = jnp.concatenate([circ[g] * older, circ[g] * newer], axis=0)
            window = product[ch, pl.ds(at, 2 * LONG)]
            w = jnp.dot(window, matrix, preferred_element_type=F32)
            now = product[ch, pl.ds(at + LONG, LONG)].astype(F32)
            w = w + direct[ch, :] * now
            out = query[ch, pl.ds(at, LONG)].astype(F32) * w
            gated[ch, pl.ds(at + REACH, LONG)] = out.astype(BF16)
        return 0

    lax.fori_loop(0, BLOCKS, long, 0)


def place(limit, k, pick, gated):
    at = k * SPILL
    if not isinstance(k, int):
        at = pl.multiple_of(at, SPILL)
    block = gated[:, pl.ds(at, 3 * SPILL)]
    moved = lax.dot_general(
        pick[...], block, (((1,), (1,)), ((), ())), preferred_element_type=F32
    )
    mine = iota((SPILL, WIDE), 0) + k * SPILL < limit
    return jnp.where(mine, moved, 0.0).astype(BF16)


N_MP = 8
SIDE = 4
DEPTH = 4 * WIDE
COLS = 1024
ROWS_W = WIDE
HALF = TOK // 2
PIECES = 2 * CHUNKS


def position():
    seq = lax.axis_index("seq")
    return seq, lax.axis_index("mp"), seq // 8, (seq // 2) % SIDE, seq % 2


def seq_at(y, x, core):
    return ((y % SIDE) * SIDE + x % SIDE) * 2 + core


class Links:
    def __init__(self, held, weight, left, right, sems):
        self.held, self.weight, self.left, self.right = held, weight, left, right
        (self.zs, self.zr, self.xs, self.xr, self.ys, self.yr, self.cs, self.cr, self.ss, self.sr) = sems
        self.seq, self.mp, self.y, self.x, self.core = position()

    def greet(self):
        barrier = pltpu.get_barrier_semaphore()
        targets = [{"mp": (self.mp + d) % N_MP} for d in (1, N_MP - 1)]
        targets += [{"seq": (self.seq + d) % 32} for d in (1, 31)]
        targets += [{"seq": seq_at(self.y, self.x + d, self.core)} for d in (1, SIDE - 1)]
        targets += [{"seq": seq_at(self.y + d, self.x, self.core)} for d in (1, SIDE - 1)]
        targets += [{"seq": seq_at(self.y, self.x, 1 - self.core)}]
        for target in targets:
            pl.semaphore_signal(barrier, inc=1, device_id=target, device_id_type=MESH)

    def meet(self):
        pl.semaphore_wait(pltpu.get_barrier_semaphore(), 9)

    def z_copy(self, way, step, piece):
        src = (self.mp + (N_MP - step if way == 0 else step)) % N_MP
        ref = self.held.at[src, piece % 2, piece // 2]
        to = (self.mp + (1 if way == 0 else N_MP - 1)) % N_MP
        return pltpu.make_async_remote_copy(
            ref, ref, self.zs.at[way, step, piece], self.zr.at[way, step, piece],
            device_id={"mp": to}, device_id_type=MESH,
        )

    def z_arrived(self, way, step, piece):
        src = (self.mp + (N_MP - step - 1 if way == 0 else step + 1)) % N_MP
        ref = self.held.at[src, piece % 2, piece // 2]
        pltpu.make_async_remote_copy(
            ref, ref, self.zs.at[way, step, piece], self.zr.at[way, step, piece],
            device_id={"mp": self.mp}, device_id_type=MESH,
        ).wait_recv()

    def w_rows(self, y, x, part):
        at = seq_at(y, x, self.core) * ROWS_W
        size = ROWS_W
        if part is not None:
            size = ROWS_W // 2
            at = at + part * size
        return self.weight.at[pl.ds(pl.multiple_of(at, size), size), :]

    def w_copy(self, send, recv, ref, to):
        return pltpu.make_async_remote_copy(
            ref, ref, send, recv, device_id={"seq": to}, device_id_type=MESH
        )

    def x_copy(self, way, step):
        d = 1 if way == 0 else SIDE - 1
        ref = self.w_rows(self.y, self.x + step * (SIDE - d), None if step == 0 else way)
        return self.w_copy(self.xs.at[way, step], self.xr.at[way, step], ref, seq_at(self.y, self.x + d, self.core))

    def x_arrived(self, way, step):
        d = 1 if way == 0 else SIDE - 1
        ref = self.w_rows(self.y, self.x + (step + 1) * (SIDE - d), None if step == 0 else way)
        self.w_copy(self.xs.at[way, step], self.xr.at[way, step], ref, self.seq).wait_recv()

    def y_copy(self, way, step, dx):
        d = 1 if way == 0 else SIDE - 1
        ref = self.w_rows(self.y + step * (SIDE - d), self.x + dx, None if step == 0 else way)
        return self.w_copy(
            self.ys.at[way, step, dx], self.yr.at[way, step, dx], ref, seq_at(self.y + d, self.x, self.core)
        )

    def y_arrived(self, way, step, dx):
        d = 1 if way == 0 else SIDE - 1
        ref = self.w_rows(self.y + (step + 1) * (SIDE - d), self.x + dx, None if step == 0 else way)
        self.w_copy(self.ys.at[way, step, dx], self.yr.at[way, step, dx], ref, self.seq).wait_recv()

    def c_copy(self, dy, dx):
        ref = self.w_rows(self.y + dy, self.x + dx, None)
        return self.w_copy(
            self.cs.at[dy, dx], self.cr.at[dy, dx], ref, seq_at(self.y, self.x, 1 - self.core)
        )

    def c_arrived(self, dy, dx):
        at = seq_at(self.y + dy, self.x + dx, 1 - self.core) * ROWS_W
        ref = self.weight.at[pl.ds(pl.multiple_of(at, ROWS_W), ROWS_W), :]
        self.w_copy(self.cs.at[dy, dx], self.cr.at[dy, dx], ref, self.seq).wait_recv()

    def s_copy(self, way, chunk, ref):
        into = (self.left if way == 0 else self.right).at[chunk]
        to = (self.seq + (1 if way == 0 else 31)) % 32
        return pltpu.make_async_remote_copy(
            ref, into, self.ss.at[way, chunk], self.sr.at[way, chunk],
            device_id={"seq": to}, device_id_type=MESH,
        )

    def w_begin(self):
        for way in (0, 1):
            self.x_copy(way, 0).start()
            self.y_copy(way, 0, 0).start()
        self.c_copy(0, 0).start()

    def w_row(self):
        for way, dx in ((0, SIDE - 1), (1, 1)):
            self.x_arrived(way, 0)
            self.x_copy(way, 1).start()
            for to in (0, 1):
                self.y_copy(to, 0, dx).start()
            self.c_copy(0, dx).start()

    def w_far(self):
        for way in (0, 1):
            self.x_arrived(way, 1)
        for to in (0, 1):
            self.y_copy(to, 0, 2).start()
        self.c_copy(0, 2).start()

    def w_near(self, dx):
        for way, dy in ((0, SIDE - 1), (1, 1)):
            self.y_arrived(way, 0, dx)
            self.y_copy(way, 1, dx).start()
            self.c_copy(dy, dx).start()

    def w_last(self, dx):
        for way in (0, 1):
            self.y_arrived(way, 1, dx)
        self.c_copy(2, dx).start()

    def w_end(self):
        for dy in range(SIDE):
            for dx in range(SIDE):
                self.c_arrived(dy, dx)

    def relay(self, step, piece0, piece1):
        self.z_arrived(0, step - 1, piece0)
        self.z_copy(0, step, piece0).start()
        self.z_arrived(1, step - 1, piece1)
        self.z_copy(1, step, piece1).start()

    def leave(self):
        for way in (0, 1):
            for step in range(2):
                self.x_copy(way, step).wait_send()
                for dx in range(SIDE):
                    self.y_copy(way, step, dx).wait_send()

            def drain(n, _):
                self.z_copy(way, n // PIECES, n % PIECES).wait_send()
                return 0

            lax.fori_loop(0, 3 * PIECES, drain, 0)
            for piece in range(CHUNKS):
                self.z_copy(way, 3, piece + way * CHUNKS).wait_send()
        for dy in range(SIDE):
            for dx in range(SIDE):
                self.c_copy(dy, dx).wait_send()


COLS_STEP = 256


def part_product(held, weight, src, half, chunks, cols):
    lhs = jnp.concatenate([held[src, half, q] for q in chunks], axis=1)
    rhs = jnp.concatenate(
        [weight[pl.ds(pl.multiple_of((src * CHUNKS + q) * WIDE, WIDE), WIDE), cols] for q in chunks], axis=0
    )
    return jnp.dot(lhs, rhs, preferred_element_type=F32)


def columns(n):
    return pl.ds(pl.multiple_of(n * COLS_STEP, COLS_STEP), COLS_STEP)


def add_product(held, weight, total, src, half, chunks):
    def body(n, _):
        cols = columns(n)
        total[half, :, cols] += part_product(held, weight, src, half, chunks, cols)
        return 0

    lax.fori_loop(0, COLS // COLS_STEP, body, 0)


def finish(held, weight, total, staged, src, half, chunks):
    def body(n, _):
        cols = columns(n)
        value = total[half, :, cols] + part_product(held, weight, src, half, chunks, cols)
        staged[half, :, cols] = value.astype(BF16)
        return 0

    lax.fori_loop(0, COLS // COLS_STEP, body, 0)


def source_of(mp, u):
    p = u // 2
    far = (p + 1) // 2
    return (mp + N_MP + far * (1 - 2 * (p % 2))) % N_MP


def add_sources(held, weight, total, mp, low, high):
    def body(u, _):
        add_product(held, weight, total, source_of(mp, u), u % 2, range(CHUNKS))
        return 0

    lax.fori_loop(low, high, body, 0)


def mix_kernel(projections, own_weight, offsets, owners, short_filter, long_filter, skip, out, *scratch):
    panels, masks, later, near, taps, pick, circ, direct, query, product, gated = scratch[:11]
    mine, outgoing, held, weight, total, staged, left, right, in_sem, own_sem, out_sem = scratch[11:22]
    links = Links(held, weight, left, right, scratch[22:])
    mp = links.mp

    def fetch(q):
        return pltpu.make_async_copy(
            projections.at[:, pl.ds(pl.multiple_of(q * WIDE, WIDE), WIDE), :], panels.at[q], in_sem.at[q]
        )

    own = pltpu.make_async_copy(own_weight, links.w_rows(links.y, links.x, None), own_sem)
    own.start()
    for q in range(CHUNKS):
        fetch(q).start()
    links.greet()
    limit = prepare(
        links.seq, mp, offsets, owners, short_filter, long_filter, masks, later, near, taps, pick, product, gated
    )
    total[...] = jnp.zeros_like(total)
    links.meet()
    own.wait()
    links.w_begin()

    def spill(way, q):
        return links.s_copy(way, q, outgoing.at[q, way])

    def edges(q):
        for way in (0, 1):
            spill(way, q).wait_recv()
        held[mp, 1, q, 0:SPILL] = mine[0] + left[q]
        held[mp, 1, q, SPILL : 2 * SPILL] = mine[1] + right[q]
        for way in (0, 1):
            links.z_copy(way, 0, 2 * q + 1).start()

    def chunk(q, _):
        fetch(q).wait()
        short_stage(mp, q, panels, near, skip, later, taps, circ, direct, query, product)

        @pl.when(q >= 1)
        def _():
            edges(q - 1)
            links.relay(1, 2 * q - 2, 2 * q - 2)

        for n, step in ((1, links.w_row), (2, lambda: links.w_near(0)), (3, lambda: links.w_near(1))):
            pl.when(q == n)(step)
        long_stage(masks, circ, direct, query, product, gated)
        outgoing[q, 0] = place(limit, 5, pick, gated)
        outgoing[q, 1] = place(limit, 0, pick, gated)
        for way in (0, 1):
            spill(way, q).start()
        held[mp, 0, q, 0:SPILL] = place(limit, 2, pick, gated)
        held[mp, 0, q, SPILL : 2 * SPILL] = place(limit, 3, pick, gated)
        for way in (0, 1):
            links.z_copy(way, 0, 2 * q).start()
        mine[0] = place(limit, 1, pick, gated)
        mine[1] = place(limit, 4, pick, gated)

        @pl.when(q >= 1)
        def _():
            links.relay(1, 2 * q - 1, 2 * q - 1)

        for n, step in (
            (1, links.w_far), (2, lambda: links.w_near(SIDE - 1)), (3, lambda: links.w_near(2))
        ):
            pl.when(q == n)(step)
        return 0

    lax.fori_loop(0, CHUNKS, chunk, 0)
    edges(CHUNKS - 1)
    for k in (PIECES - 2, PIECES - 1):
        links.relay(1, k, k)
    for k in range(PIECES):
        links.relay(2, k, k)
        if k < SIDE:
            links.w_last((0, SIDE - 1, 1, 2)[k])
        if k == SIDE:
            links.w_end()
    add_sources(held, weight, total, mp, 0, 6)
    for k in range(CHUNKS):
        links.relay(3, k, k + CHUNKS)
    add_sources(held, weight, total, mp, 6, 10)
    for k in range(CHUNKS):
        links.z_arrived(0, 2, k + CHUNKS)
        links.z_arrived(1, 2, k)
    add_sources(held, weight, total, mp, 10, 14)
    far = (mp + N_MP // 2) % N_MP
    for half in (0, 1):
        links.z_arrived(0, 3, half)
        links.z_arrived(1, 3, half + CHUNKS)
        add_product(held, weight, total, far, half, (0, 2))
    writes = []
    for half in (0, 1):
        links.z_arrived(0, 3, 2 + half)
        links.z_arrived(1, 3, 2 + half + CHUNKS)
        finish(held, weight, total, staged, far, half, (1, 3))
        if half == 0:
            spans = ((0, HALF, SPILL),)
        else:
            spans = ((0, SPILL, 0), (SPILL, HALF, TOK - SPILL))
        for n, (low, high, at) in enumerate(spans):
            copy = pltpu.make_async_copy(
                staged.at[half, low:high], out.at[at : at + high - low], out_sem.at[half, n]
            )
            copy.start()
            writes.append(copy)
    for q in range(CHUNKS):
        for way in (0, 1):
            spill(way, q).wait_send()
    links.leave()
    for copy in writes:
        copy.wait()


FILTER_SCRATCH = [
    pltpu.VMEM((CHUNKS, 3, WIDE, CAP), BF16),
    pltpu.VMEM((BLOCKS, 2 * LONG, LONG), BF16),
    pltpu.VMEM((SHORT - 1, 8, CAP), F32),
    pltpu.VMEM((3, WIDE, WIDE), F32),
    pltpu.VMEM((CHUNKS * GROUPS, LONG), F32),
    pltpu.VMEM((SPILL, 3 * SPILL), BF16),
    pltpu.VMEM((GROUPS, LONG, LONG), BF16),
    pltpu.VMEM((WIDE, WIDE), F32),
    pltpu.VMEM((WIDE, CAP), BF16),
    pltpu.VMEM((WIDE, LONG + CAP), BF16),
    pltpu.VMEM((WIDE, REACH + CAP), BF16),
    pltpu.VMEM((2, SPILL, WIDE), BF16),
    pltpu.VMEM((CHUNKS, 2, SPILL, WIDE), BF16),
]
LINK_SCRATCH = [
    pltpu.VMEM((N_MP, 2, CHUNKS, HALF, WIDE), BF16),
    pltpu.VMEM((N_MP * DEPTH, COLS), BF16),
    pltpu.VMEM((2, HALF, COLS), F32),
    pltpu.VMEM((2, HALF, COLS), BF16),
    pltpu.VMEM((CHUNKS, SPILL, WIDE), BF16),
    pltpu.VMEM((CHUNKS, SPILL, WIDE), BF16),
    pltpu.SemaphoreType.DMA((CHUNKS,)),
    pltpu.SemaphoreType.DMA,
    pltpu.SemaphoreType.DMA((2, 2)),
    pltpu.SemaphoreType.DMA((2, 4, PIECES)),
    pltpu.SemaphoreType.DMA((2, 4, PIECES)),
    pltpu.SemaphoreType.DMA((2, 2)),
    pltpu.SemaphoreType.DMA((2, 2)),
    pltpu.SemaphoreType.DMA((2, 2, SIDE)),
    pltpu.SemaphoreType.DMA((2, 2, SIDE)),
    pltpu.SemaphoreType.DMA((SIDE, SIDE)),
    pltpu.SemaphoreType.DMA((SIDE, SIDE)),
    pltpu.SemaphoreType.DMA((2, CHUNKS)),
    pltpu.SemaphoreType.DMA((2, CHUNKS)),
]


def per_device(projections, lengths, owners, offsets, short_filter, long_filter, skip, out_weight):
    vmem = pl.BlockSpec(memory_space=pltpu.VMEM)
    anywhere = pl.BlockSpec(memory_space=pl.ANY)
    return pl.pallas_call(
        mix_kernel,
        out_shape=jax.ShapeDtypeStruct((TOK, COLS), BF16),
        in_specs=[anywhere, anywhere] + [vmem] * 5,
        out_specs=anywhere,
        scratch_shapes=FILTER_SCRATCH + LINK_SCRATCH,
        compiler_params=pltpu.CompilerParams(
            collective_id=0, has_side_effects=True, vmem_limit_bytes=60 * 2**20
        ),
    )(
        projections,
        out_weight,
        offsets.reshape(1, -1),
        owners.reshape(1, -1),
        short_filter.transpose(0, 2, 1),
        long_filter,
        skip.reshape(-1, WIDE),
    )


def solution(mesh):
    placed = (P(None, "mp", "seq"), P(), P(), P(), P(), P(), P(), P("seq", "mp"))
    return jax.shard_map(
        per_device, mesh=mesh, in_specs=placed, out_specs=P("seq", "mp"), check_vma=False
    )
```

```python
import functools

import jax
import jax.numpy as jnp
from jax import lax
from jax.experimental import pallas as pl
from jax.experimental.pallas import tpu as pltpu
from jax.sharding import PartitionSpec as P

MESH = pl.DeviceIdType.MESH
F32 = jnp.float32
BF16 = jnp.bfloat16

GSIZE = 16
SHORT = 7
LONG = 128
TOK = 1024
SPILL = 256
CAP = 1536
TOKENS = 32768
WIDE = 128
CHUNKS = 4
GROUPS = WIDE // GSIZE
BLOCKS = CAP // LONG
REACH = 2 * SPILL


def iota(shape, dim):
    return lax.broadcasted_iota(jnp.int32, shape, dim)


def prepare(seq, model, offsets, owners, short_filter, long_filter, masks, later, near, taps, pick, product, gated):
    off = offsets[...]
    own = owners[...]
    first = jnp.min(jnp.where(own == seq, off, TOKENS), axis=1, keepdims=True)
    after = jnp.min(jnp.where(own == seq + 1, off, TOKENS), axis=1, keepdims=True)
    shift = first - seq * TOK + SPILL
    column = jnp.broadcast_to(off, (LONG, LONG)).T
    lag = iota((LONG, LONG), 1) - iota((LONG, LONG), 0)
    older = jnp.where(lag < 0, lag + LONG, TOKENS)
    newer = jnp.where(lag >= 0, lag, TOKENS)
    for b in range(BLOCKS):
        token = first + iota((1, LONG), 1) + b * LONG
        begin = jnp.max(jnp.where(column <= token, column, 0), axis=0, keepdims=True)
        pos = jnp.broadcast_to(token - begin, (8, LONG))
        wide = jnp.broadcast_to(token - begin, (LONG, LONG))
        masks[b, 0:LONG, :] = jnp.where(older <= wide, 1.0, 0.0).astype(BF16)
        masks[b, LONG : 2 * LONG, :] = jnp.where(newer <= wide, 1.0, 0.0).astype(BF16)
        for j in range(1, SHORT):
            later[j - 1, :, b * LONG : (b + 1) * LONG] = jnp.where(pos >= j, 1.0, 0.0)
    rows = CHUNKS * GROUPS
    taps[...] = long_filter[pl.ds(pl.multiple_of(model * rows, rows), rows), :].astype(F32)
    aside = pl.ds(pl.multiple_of(model // 4 * WIDE, WIDE), WIDE)
    for p in range(3):
        block = jnp.concatenate([short_filter[p, :, aside], jnp.zeros((WIDE - SHORT, WIDE), F32)], axis=0)
        near[p] = block.T
    turned = iota((SPILL, 3 * SPILL), 1) - iota((SPILL, 3 * SPILL), 0) - REACH
    pick[...] = jnp.where(turned == -shift, 1.0, 0.0).astype(BF16)
    product[:, 0:LONG] = jnp.zeros((WIDE, LONG), BF16)
    gated[:, 0:REACH] = jnp.zeros((WIDE, REACH), BF16)
    return after - first + shift


def short_stage(model, chunk, low_block, high_block, panels, near, skip, later, taps, circ, direct, query, product):
    row = model % 4 * (CHUNKS * GROUPS) + chunk * GROUPS
    if low_block == 0:
        gains = skip[pl.ds(model * CHUNKS + chunk, 1), :]
        direct[...] = jnp.broadcast_to(gains, (WIDE, WIDE)).T
    lane = iota((GSIZE, LONG), 1)

    def short(g, _):
        ch = pl.ds(pl.multiple_of(g * GSIZE, GSIZE), GSIZE)
        if low_block == 0:
            line = jnp.broadcast_to(taps[pl.ds(chunk * GROUPS + g, 1), :], (LONG, LONG))
            circ[g] = pltpu.roll(line, 0, 1, stride=1, stride_axis=0).astype(BF16)
        factor = []
        for p in range(3):
            f = near[p, pl.ds(row + g, 1), :]
            factor.append([jnp.broadcast_to(f[:, j : j + 1], (8, LONG)) for j in range(SHORT)])
        rolled = [[None] * SHORT for _ in range(3)]
        if low_block > 0:
            at = slice((low_block - 1) * LONG, low_block * LONG)
            rolled = [[pltpu.roll(panels[chunk, p, ch, at], j, 1) for j in range(SHORT)] for p in range(3)]
        for b in range(low_block, high_block):
            at = slice(b * LONG, (b + 1) * LONG)
            sums = []
            for p in range(3):
                x = panels[chunk, p, ch, at]
                wide = x.astype(F32)
                low = factor[p][0] * wide[0:8]
                high = factor[p][0] * wide[8:16]
                for j in range(1, SHORT):
                    turned = pltpu.roll(x, j, 1)
                    before = rolled[p][j]
                    rolled[p][j] = turned
                    if b > 0:
                        turned = jnp.where(lane < j, before, turned)
                    weight = factor[p][j] * later[j - 1, :, at]
                    wide = turned.astype(F32)
                    low = low + weight * wide[0:8]
                    high = high + weight * wide[8:16]
                sums.append(jnp.concatenate([low, high], axis=0))
            query[ch, at] = sums[0].astype(BF16)
            product[ch, (b + 1) * LONG : (b + 2) * LONG] = (sums[1] * sums[2]).astype(BF16)
        return 0

    lax.fori_loop(0, GROUPS, short, 0)


def long_stage(low_block, high_block, masks, circ, direct, query, product, gated):
    def long(b, _):
        at = pl.multiple_of(b * LONG, LONG)
        older = masks[b, 0:LONG, :]
        newer = masks[b, LONG : 2 * LONG, :]
        for g in range(GROUPS):
            ch = slice(g * GSIZE, (g + 1) * GSIZE)
            matrix = jnp.concatenate([circ[g] * older, circ[g] * newer], axis=0)
            window = product[ch, pl.ds(at, 2 * LONG)]
            w = jnp.dot(window, matrix, preferred_element_type=F32)
            now = product[ch, pl.ds(at + LONG, LONG)].astype(F32)
            w = w + direct[ch, :] * now
            out = query[ch, pl.ds(at, LONG)].astype(F32) * w
            gated[ch, pl.ds(at + REACH, LONG)] = out.astype(BF16)
        return 0

    lax.fori_loop(low_block, high_block, long, 0)


def place(limit, k, pick, gated):
    at = k * SPILL
    if not isinstance(k, int):
        at = pl.multiple_of(at, SPILL)
    block = gated[:, pl.ds(at, 3 * SPILL)]
    moved = lax.dot_general(
        pick[...], block, (((1,), (1,)), ((), ())), preferred_element_type=F32
    )
    mine = iota((SPILL, WIDE), 0) + k * SPILL < limit
    return jnp.where(mine, moved, 0.0).astype(BF16)


N_MP = 8
SIDE = 4
DEPTH = 4 * WIDE
COLS = 1024
ROWS_W = WIDE
HALF = TOK // 2
PIECES = 2 * CHUNKS


def position():
    seq = lax.axis_index("seq")
    return seq, lax.axis_index("mp"), seq // 8, (seq // 2) % SIDE, seq % 2


def seq_at(y, x, core):
    return ((y % SIDE) * SIDE + x % SIDE) * 2 + core


class Links:
    def __init__(self, held, weight, left, right, sems):
        self.held, self.weight, self.left, self.right = held, weight, left, right
        (self.zs, self.zf, self.zr, self.ws, self.xr, self.yr, self.cr, self.ss, self.sr) = sems
        self.seq, self.mp, self.y, self.x, self.core = position()

    def greet(self):
        barrier = pltpu.get_barrier_semaphore()
        targets = [{"mp": (self.mp + d) % N_MP} for d in (1, N_MP - 1)]
        targets += [{"seq": (self.seq + d) % 32} for d in (1, 31)]
        targets += [{"seq": seq_at(self.y, self.x + d, self.core)} for d in (1, SIDE - 1)]
        targets += [{"seq": seq_at(self.y + d, self.x, self.core)} for d in (1, SIDE - 1)]
        targets += [{"seq": seq_at(self.y, self.x, 1 - self.core)}]
        for target in targets:
            pl.semaphore_signal(barrier, inc=1, device_id=target, device_id_type=MESH)

    def meet(self):
        pl.semaphore_wait(pltpu.get_barrier_semaphore(), 9)

    def z_push(self, way, ref, recv, late=0):
        to = (self.mp + (1 if way == 0 else N_MP - 1)) % N_MP
        pltpu.make_async_remote_copy(
            ref, ref, self.zs.at[way, late], recv, device_id={"mp": to}, device_id_type=MESH
        ).start()

    def z_take(self, ref, recv):
        pltpu.make_async_copy(ref, ref, recv).wait()

    def own_part(self, src, chunk, part):
        if part == 2:
            return self.held.at[src, 1, chunk]
        return self.held.at[src, 0, chunk, part * SPILL : (part + 1) * SPILL]

    def z_begin(self, chunk, part):
        for way in (0, 1):
            self.z_push(way, self.own_part(self.mp, chunk, part), self.zf.at[way, chunk, part])

    def behind(self, way, step):
        return (self.mp + (N_MP - step if way == 0 else step)) % N_MP

    def z_first(self, chunk, parts):
        for way in (0, 1):
            src = self.behind(way, 1)
            for part in parts:
                self.z_take(self.own_part(src, chunk, part), self.zf.at[way, chunk, part])
            half = parts[-1] // 2
            self.z_push(way, self.held.at[src, half, chunk], self.zr.at[way, 0, 2 * chunk + half])

    def z_ref(self, way, step, piece):
        return self.held.at[self.behind(way, step + 1), piece % 2, piece // 2]

    def z_arrived(self, way, step, piece):
        self.z_take(self.z_ref(way, step, piece), self.zr.at[way, step - 1, piece])

    def relay(self, way, step, pieces):
        late = 1 if step == 3 else 0
        for piece in pieces:
            self.z_arrived(way, step - 1, piece)
            self.z_push(way, self.z_ref(way, step - 1, piece), self.zr.at[way, step - 1, piece], late)

    def w_rows(self, y, x, part):
        at = seq_at(y, x, self.core) * ROWS_W
        size = ROWS_W
        if part is not None:
            size = ROWS_W // 2
            at = at + part * size
        return self.weight.at[pl.ds(pl.multiple_of(at, size), size), :]

    def w_copy(self, send, recv, ref, to):
        return pltpu.make_async_remote_copy(
            ref, ref, send, recv, device_id={"seq": to}, device_id_type=MESH
        )

    def x_copy(self, way, step):
        d = 1 if way == 0 else SIDE - 1
        ref = self.w_rows(self.y, self.x + step * (SIDE - d), None if step == 0 else way)
        return self.w_copy(self.ws, self.xr.at[way, step], ref, seq_at(self.y, self.x + d, self.core))

    def x_arrived(self, way, step):
        d = 1 if way == 0 else SIDE - 1
        ref = self.w_rows(self.y, self.x + (step + 1) * (SIDE - d), None if step == 0 else way)
        self.z_take(ref, self.xr.at[way, step])

    def y_copy(self, way, step, dx):
        d = 1 if way == 0 else SIDE - 1
        ref = self.w_rows(self.y + step * (SIDE - d), self.x + dx, None if step == 0 else way)
        return self.w_copy(
            self.ws, self.yr.at[way, step, dx], ref, seq_at(self.y + d, self.x, self.core)
        )

    def y_arrived(self, way, step, dx):
        d = 1 if way == 0 else SIDE - 1
        ref = self.w_rows(self.y + (step + 1) * (SIDE - d), self.x + dx, None if step == 0 else way)
        self.z_take(ref, self.yr.at[way, step, dx])

    def c_copy(self, dy, dx):
        ref = self.w_rows(self.y + dy, self.x + dx, None)
        return self.w_copy(
            self.ws, self.cr.at[dy, dx], ref, seq_at(self.y, self.x, 1 - self.core)
        )

    def c_arrived(self, dy, dx):
        at = seq_at(self.y + dy, self.x + dx, 1 - self.core) * ROWS_W
        ref = self.weight.at[pl.ds(pl.multiple_of(at, ROWS_W), ROWS_W), :]
        self.z_take(ref, self.cr.at[dy, dx])

    def s_copy(self, way, chunk, ref):
        into = (self.left if way == 0 else self.right).at[chunk]
        to = (self.seq + (1 if way == 0 else 31)) % 32
        return pltpu.make_async_remote_copy(
            ref, into, self.ss, self.sr.at[way, chunk],
            device_id={"seq": to}, device_id_type=MESH,
        )

    def w_begin(self):
        for way in (0, 1):
            self.x_copy(way, 0).start()
            self.y_copy(way, 0, 0).start()
        self.c_copy(0, 0).start()

    def w_row(self):
        for way, dx in ((0, SIDE - 1), (1, 1)):
            self.x_arrived(way, 0)
            self.x_copy(way, 1).start()
            for to in (0, 1):
                self.y_copy(to, 0, dx).start()
            self.c_copy(0, dx).start()

    def w_far(self):
        for way in (0, 1):
            self.x_arrived(way, 1)
        for to in (0, 1):
            self.y_copy(to, 0, 2).start()
        self.c_copy(0, 2).start()

    def w_near(self, dx):
        for way, dy in ((0, SIDE - 1), (1, 1)):
            self.y_arrived(way, 0, dx)
            self.y_copy(way, 1, dx).start()
            self.c_copy(dy, dx).start()

    def w_last(self, dx):
        for way in (0, 1):
            self.y_arrived(way, 1, dx)
        self.c_copy(2, dx).start()

    def w_end(self):
        for dy in range(SIDE):
            for dx in range(SIDE):
                self.c_arrived(dy, dx)

    def leave(self):
        for way in (0, 1):
            ref = self.held.at[0 : N_MP // 2 - 1]
            self.z_take(ref, self.zs.at[way, 0])
            self.z_take(self.held.at[0, 0], self.zs.at[way, 1])
        sent = (2 + 2 * SIDE) * (ROWS_W + ROWS_W // 2) + SIDE * SIDE * ROWS_W
        self.z_take(self.weight.at[0:sent], self.ws)
        self.z_take(self.held.at[0, 0], self.ss)


COLS_STEP = 256


def part_product(held, weight, src, half, chunks, cols):
    lhs = jnp.concatenate([held[src, half, q] for q in chunks], axis=1)
    rhs = jnp.concatenate(
        [weight[pl.ds(pl.multiple_of((src * CHUNKS + q) * WIDE, WIDE), WIDE), cols] for q in chunks], axis=0
    )
    return jnp.dot(lhs, rhs, preferred_element_type=F32)


def columns(n):
    return pl.ds(pl.multiple_of(n * COLS_STEP, COLS_STEP), COLS_STEP)


def add_product(held, weight, total, src, half, chunks, fresh=False):
    def body(n, _):
        cols = columns(n)
        value = part_product(held, weight, src, half, chunks, cols)
        if fresh:
            total[half, :, cols] = value
        else:
            total[half, :, cols] += value
        return 0

    lax.fori_loop(0, COLS // COLS_STEP, body, 0)


def finish(held, weight, total, out, src, half, chunks):
    def body(n, _):
        cols = columns(n)
        value = (total[half, :, cols] + part_product(held, weight, src, half, chunks, cols)).astype(BF16)
        if half == 0:
            out[SPILL : SPILL + HALF, cols] = value
        else:
            out[0:SPILL, cols] = value[0:SPILL]
            out[TOK - SPILL : TOK, cols] = value[SPILL:]
        return 0

    lax.fori_loop(0, COLS // COLS_STEP, body, 0)


def source_of(mp, u):
    p = u // 2
    far = (p + 1) // 2
    return (mp + N_MP + far * (1 - 2 * (p % 2))) % N_MP


def add_sources(held, weight, total, mp, low, high):
    def body(u, _):
        add_product(held, weight, total, source_of(mp, u), u % 2, range(CHUNKS))
        return 0

    lax.fori_loop(low, high, body, 0)


SEGMENTS = ((0, 6), (6, 8), (8, BLOCKS))


def mix_kernel(projections, own_weight, offsets, owners, short_filter, long_filter, skip, out, *scratch):
    panels, masks, later, near, taps, pick, circ, direct, query, product, gated = scratch[:11]
    mine, outgoing, held, weight, total, left, right, in_sem, own_sem = scratch[11:20]
    links = Links(held, weight, left, right, scratch[20:])
    mp = links.mp

    def fetch(q):
        return pltpu.make_async_copy(
            projections.at[:, pl.ds(pl.multiple_of(q * WIDE, WIDE), WIDE), :], panels.at[q], in_sem.at[q]
        )

    own = pltpu.make_async_copy(own_weight, links.w_rows(links.y, links.x, None), own_sem)
    links.greet()
    fetch(0).start()
    own.start()
    for q in range(1, CHUNKS):
        fetch(q).start()
    limit = prepare(
        links.seq, mp, offsets, owners, short_filter, long_filter, masks, later, near, taps, pick, product, gated
    )
    own.wait()

    def spill(way, q):
        return links.s_copy(way, q, outgoing.at[q, way])

    def edges(q):
        for way in (0, 1):
            into = (left if way == 0 else right).at[q]
            links.z_take(into, links.sr.at[way, q])
        held[mp, 1, q, 0:SPILL] = mine[0] + left[q]
        held[mp, 1, q, SPILL : 2 * SPILL] = mine[1] + right[q]
        links.z_begin(q, 2)

    def stages(q, segment):
        low, high = SEGMENTS[segment]
        short_stage(mp, q, low, high, panels, near, skip, later, taps, circ, direct, query, product)
        long_stage(low, high, masks, circ, direct, query, product, gated)

    def weight_steps(q, steps):
        for n, step in steps:
            pl.when(q == n)(step)

    def opening(q):
        fetch(q).wait()
        stages(q, 0)
        held[mp, 0, q, 0:SPILL] = place(limit, 2, pick, gated)

    opening(0)
    links.meet()
    links.z_begin(0, 0)
    links.w_begin()

    def chunk(q, _):
        stages(q, 1)
        held[mp, 0, q, SPILL : 2 * SPILL] = place(limit, 3, pick, gated)
        links.z_begin(q, 1)
        stages(q, 2)
        outgoing[q, 0] = place(limit, 5, pick, gated)
        outgoing[q, 1] = place(limit, 0, pick, gated)
        for way in (0, 1):
            spill(way, q).start()
        mine[0] = place(limit, 1, pick, gated)
        mine[1] = place(limit, 4, pick, gated)

        @pl.when(q >= 1)
        def _():
            links.z_first(q - 1, (2,))

        weight_steps(
            q, ((1, links.w_far), (2, lambda: links.w_near(SIDE - 1)), (3, lambda: links.w_near(2)))
        )

        @pl.when(q < CHUNKS - 1)
        def _():
            links.z_first(q, (0, 1))
            opening(q + 1)
            links.z_begin(q + 1, 0)
            edges(q)

        weight_steps(q, ((0, links.w_row), (1, lambda: links.w_near(0)), (2, lambda: links.w_near(1))))
        return 0

    lax.fori_loop(0, CHUNKS, chunk, 0)
    links.z_first(CHUNKS - 1, (0, 1))
    edges(CHUNKS - 1)
    links.z_first(CHUNKS - 1, (2,))
    for n, dx in enumerate((0, SIDE - 1, 1, 2)):
        links.w_last(dx)
        links.relay(0, 2, (n,))
    links.relay(1, 2, range(CHUNKS, PIECES))
    links.relay(0, 2, range(CHUNKS, PIECES))
    links.relay(1, 2, range(CHUNKS))
    links.w_end()
    for half in (0, 1):
        add_product(held, weight, total, mp, half, range(CHUNKS), True)

    def mix(n, _):
        add_sources(held, weight, total, mp, 2 * n + 2, 2 * n + 4)
        for way in (0, 1):
            links.relay(way, 3, (n + way * CHUNKS,))
        return 0

    lax.fori_loop(0, CHUNKS, mix, 0)
    for half in (0, 1):
        for k in (0, 2):
            links.z_arrived(0, 2, k + CHUNKS + half)
            links.z_arrived(1, 2, k + half)
        for d in (3, N_MP - 3):
            add_product(held, weight, total, (mp + d) % N_MP, half, range(CHUNKS))
    far = (mp + N_MP // 2) % N_MP
    for half in (0, 1):
        links.z_arrived(0, 3, half)
        links.z_arrived(1, 3, half + CHUNKS)
        add_product(held, weight, total, far, half, (0, 2))
    for half in (0, 1):
        links.z_arrived(0, 3, 2 + half)
        links.z_arrived(1, 3, 2 + half + CHUNKS)
        finish(held, weight, total, out, far, half, (1, 3))
    links.leave()


FILTER_SCRATCH = [
    pltpu.VMEM((CHUNKS, 3, WIDE, CAP), BF16),
    pltpu.VMEM((BLOCKS, 2 * LONG, LONG), BF16),
    pltpu.VMEM((SHORT - 1, 8, CAP), F32),
    pltpu.VMEM((3, WIDE, WIDE), F32),
    pltpu.VMEM((CHUNKS * GROUPS, LONG), F32),
    pltpu.VMEM((SPILL, 3 * SPILL), BF16),
    pltpu.VMEM((GROUPS, LONG, LONG), BF16),
    pltpu.VMEM((WIDE, WIDE), F32),
    pltpu.VMEM((WIDE, CAP), BF16),
    pltpu.VMEM((WIDE, LONG + CAP), BF16),
    pltpu.VMEM((WIDE, REACH + CAP), BF16),
    pltpu.VMEM((2, SPILL, WIDE), BF16),
    pltpu.VMEM((CHUNKS, 2, SPILL, WIDE), BF16),
]
LINK_SCRATCH = [
    pltpu.VMEM((N_MP, 2, CHUNKS, HALF, WIDE), BF16),
    pltpu.VMEM((N_MP * DEPTH, COLS), BF16),
    pltpu.VMEM((2, HALF, COLS), F32),
    pltpu.VMEM((CHUNKS, SPILL, WIDE), BF16),
    pltpu.VMEM((CHUNKS, SPILL, WIDE), BF16),
    pltpu.SemaphoreType.DMA((CHUNKS,)),
    pltpu.SemaphoreType.DMA,
    pltpu.SemaphoreType.DMA((2, 2)),
    pltpu.SemaphoreType.DMA((2, CHUNKS, 3)),
    pltpu.SemaphoreType.DMA((2, 3, PIECES)),
    pltpu.SemaphoreType.DMA,
    pltpu.SemaphoreType.DMA((2, 2)),
    pltpu.SemaphoreType.DMA((2, 2, SIDE)),
    pltpu.SemaphoreType.DMA((SIDE, SIDE)),
    pltpu.SemaphoreType.DMA,
    pltpu.SemaphoreType.DMA((2, CHUNKS)),
]


def per_device(projections, lengths, owners, offsets, short_filter, long_filter, skip, out_weight):
    vmem = pl.BlockSpec(memory_space=pltpu.VMEM)
    anywhere = pl.BlockSpec(memory_space=pl.ANY)
    return pl.pallas_call(
        mix_kernel,
        out_shape=pltpu.VMEM((TOK, COLS), BF16),
        in_specs=[anywhere, anywhere] + [vmem] * 5,
        out_specs=vmem,
        scratch_shapes=FILTER_SCRATCH + LINK_SCRATCH,
        compiler_params=pltpu.CompilerParams(
            collective_id=0, has_side_effects=True, vmem_limit_bytes=60 * 2**20
        ),
    )(
        projections,
        out_weight,
        offsets.reshape(1, -1),
        owners.reshape(1, -1),
        short_filter.transpose(0, 2, 1),
        long_filter,
        skip.reshape(-1, WIDE),
    )


def solution(mesh):
    placed = (P(None, "mp", "seq"), P(), P(), P(), P(), P(), P(), P("seq", "mp"))
    return jax.shard_map(
        per_device, mesh=mesh, in_specs=placed, out_specs=P("seq", "mp"), check_vma=False
    )
```

```python
import functools

import jax
import jax.numpy as jnp
from jax import lax
from jax.experimental import pallas as pl
from jax.experimental.pallas import tpu as pltpu
from jax.sharding import PartitionSpec as P

MESH = pl.DeviceIdType.MESH
F32 = jnp.float32
BF16 = jnp.bfloat16

GSIZE = 16
SHORT = 7
LONG = 128
TOK = 1024
SPILL = 256
CAP = 1536
TOKENS = 32768
WIDE = 128
CHUNKS = 4
GROUPS = WIDE // GSIZE
BLOCKS = CAP // LONG
PAD = 2 * SPILL // LONG


def iota(shape, dim):
    return lax.broadcasted_iota(jnp.int32, shape, dim)


def owner_span(seq, offsets, owners):
    off = offsets[...]
    own = owners[...]
    first = jnp.min(jnp.where(own == seq, off, TOKENS), axis=1, keepdims=True)
    after = jnp.min(jnp.where(own == seq + 1, off, TOKENS), axis=1, keepdims=True)
    shift = first - seq * TOK + SPILL
    steps = lax.shift_right_arithmetic(shift, 7)
    coarse = steps * LONG
    return first - coarse, steps, shift - coarse, after - first + shift


def mark_blocks(start, blocks, offsets, masks, later):
    column = jnp.broadcast_to(offsets[...], (LONG, LONG)).T
    lag = iota((LONG, LONG), 1) - iota((LONG, LONG), 0)
    older = jnp.where(lag < 0, lag + LONG, TOKENS)
    newer = jnp.where(lag >= 0, lag, TOKENS)
    for b in blocks:
        token = start + iota((1, LONG), 1) + b * LONG
        begin = jnp.max(jnp.where(column <= token, column, 0), axis=0, keepdims=True)
        pos = jnp.broadcast_to(token - begin, (8, LONG))
        wide = jnp.broadcast_to(token - begin, (LONG, LONG))
        masks[b, 0:LONG, :] = jnp.where(older <= wide, 1.0, 0.0).astype(BF16)
        masks[b, LONG : 2 * LONG, :] = jnp.where(newer <= wide, 1.0, 0.0).astype(BF16)
        for j in range(1, SHORT):
            later[j - 1, :, b * LONG : (b + 1) * LONG] = jnp.where(pos >= j, 1.0, 0.0)


def prepare(model, fine, short_filter, long_filter, near, taps, pick, product, gated):
    rows = CHUNKS * GROUPS
    taps[...] = long_filter[pl.ds(pl.multiple_of(model * rows, rows), rows), :].astype(F32)
    aside = pl.ds(pl.multiple_of(model // 4 * WIDE, WIDE), WIDE)
    for p in range(3):
        block = jnp.concatenate([short_filter[p, :, aside], jnp.zeros((WIDE - SHORT, WIDE), F32)], axis=0)
        near[p] = block.T
    turned = iota((SPILL, 3 * LONG), 1) - iota((SPILL, 3 * LONG), 0) - LONG
    pick[...] = jnp.where(turned == -fine, 1.0, 0.0).astype(BF16)
    product[:, :, 0:LONG] = jnp.zeros((CHUNKS, WIDE, LONG), BF16)
    gated[:, :, 0:LONG] = jnp.zeros((CHUNKS, WIDE, LONG), BF16)


def short_stage(model, chunk, ranges, fresh, coarse, panels, near, factors, skip, later, taps, circ, direct, query, product):
    if fresh:
        gains = skip[pl.ds(model * CHUNKS + chunk, 1), :]
        direct[chunk] = jnp.broadcast_to(gains, (WIDE, WIDE)).T
        first_row = pl.multiple_of(model % 4 * (CHUNKS * GROUPS) + chunk * GROUPS, GROUPS)
        for p in range(3):
            mine = near[p, pl.ds(first_row, GROUPS), :]
            for j in range(SHORT):
                factors[chunk, p * SHORT + j] = jnp.broadcast_to(mine[:, j : j + 1], (GROUPS, WIDE))
    lane = iota((GSIZE, LONG), 1)
    steps = jnp.broadcast_to(coarse, (GSIZE, LONG))

    def short(g, _):
        ch = pl.ds(pl.multiple_of(g * GSIZE, GSIZE), GSIZE)
        row = chunk * GROUPS + g

        def cells(p, b):
            x = panels[chunk, p, ch, (b + PAD) * LONG : (b + PAD + 1) * LONG]
            for k in range(1, PAD + 1):
                at = (b + PAD - k) * LONG
                x = jnp.where(steps == k, panels[chunk, p, ch, at : at + LONG], x)
            return x

        if fresh:
            line = jnp.broadcast_to(taps[pl.ds(row, 1), :], (LONG, LONG))
            circ[chunk, g] = pltpu.roll(line, 0, 1, stride=1, stride_axis=0).astype(BF16)
        factor = [
            [jnp.broadcast_to(factors[chunk, p * SHORT + j, pl.ds(g, 1), :], (8, LONG)) for j in range(SHORT)]
            for p in range(3)
        ]
        for low_block, high_block in ranges:
            rolled = [[None] * SHORT for _ in range(3)]
            if low_block > 0:
                before = [cells(p, low_block - 1) for p in range(3)]
                rolled = [[pltpu.roll(before[p], j, 1) for j in range(SHORT)] for p in range(3)]
            for b in range(low_block, high_block):
                at = slice(b * LONG, (b + 1) * LONG)
                sums = []
                for p in range(3):
                    x = cells(p, b)
                    wide = x.astype(F32)
                    low = factor[p][0] * wide[0:8]
                    high = factor[p][0] * wide[8:16]
                    for j in range(1, SHORT):
                        turned = pltpu.roll(x, j, 1)
                        before = rolled[p][j]
                        rolled[p][j] = turned
                        if b > 0:
                            turned = jnp.where(lane < j, before, turned)
                        weight = factor[p][j] * later[j - 1, :, at]
                        wide = turned.astype(F32)
                        low = low + weight * wide[0:8]
                        high = high + weight * wide[8:16]
                    sums.append(jnp.concatenate([low, high], axis=0))
                query[chunk, ch, at] = sums[0].astype(BF16)
                product[chunk, ch, (b + 1) * LONG : (b + 2) * LONG] = (sums[1] * sums[2]).astype(BF16)
        return 0

    lax.fori_loop(0, GROUPS, short, 0)


def long_stage(chunk, low_block, high_block, masks, circ, direct, query, product, gated):
    def long(b, _):
        at = pl.multiple_of(b * LONG, LONG)
        older = masks[b, 0:LONG, :]
        newer = masks[b, LONG : 2 * LONG, :]
        for g in range(GROUPS):
            ch = slice(g * GSIZE, (g + 1) * GSIZE)
            matrix = jnp.concatenate([circ[chunk, g] * older, circ[chunk, g] * newer], axis=0)
            window = product[chunk, ch, pl.ds(at, 2 * LONG)]
            w = jnp.dot(window, matrix, preferred_element_type=F32)
            now = product[chunk, ch, pl.ds(at + LONG, LONG)].astype(F32)
            w = w + direct[chunk, ch, :] * now
            out = query[chunk, ch, pl.ds(at, LONG)].astype(F32) * w
            gated[chunk, ch, pl.ds(at + LONG, LONG)] = out.astype(BF16)
        return 0

    lax.fori_loop(low_block, high_block, long, 0)


def place(limit, chunk, k, pick, gated):
    at = k * SPILL
    if not isinstance(k, int):
        at = pl.multiple_of(at, SPILL)
    block = gated[chunk, :, pl.ds(at, 3 * LONG)]
    moved = lax.dot_general(
        pick[...], block, (((1,), (1,)), ((), ())), preferred_element_type=F32
    )
    mine = iota((SPILL, WIDE), 0) + k * SPILL < limit
    return jnp.where(mine, moved, 0.0).astype(BF16)


N_MP = 8
SIDE = 4
DEPTH = 4 * WIDE
COLS = 1024
ROWS_W = WIDE
HALF = TOK // 2
PIECES = 2 * CHUNKS


def position():
    seq = lax.axis_index("seq")
    return seq, lax.axis_index("mp"), seq // 8, (seq // 2) % SIDE, seq % 2


def seq_at(y, x, core):
    return ((y % SIDE) * SIDE + x % SIDE) * 2 + core


class Links:
    def __init__(self, held, weight, left, right, sems):
        self.held, self.weight, self.left, self.right = held, weight, left, right
        (self.zs, self.zf, self.zr, self.ws, self.xr, self.yr, self.cr, self.ss, self.sr) = sems
        self.seq, self.mp, self.y, self.x, self.core = position()

    def greet(self):
        barrier = pltpu.get_barrier_semaphore()
        targets = [{"mp": (self.mp + d) % N_MP} for d in (1, N_MP - 1)]
        targets += [{"seq": (self.seq + d) % 32} for d in (1, 31)]
        targets += [{"seq": seq_at(self.y, self.x + d, self.core)} for d in (1, SIDE - 1)]
        targets += [{"seq": seq_at(self.y + d, self.x, self.core)} for d in (1, SIDE - 1)]
        targets += [{"seq": seq_at(self.y, self.x, 1 - self.core)}]
        for target in targets:
            pl.semaphore_signal(barrier, inc=1, device_id=target, device_id_type=MESH)

    def meet(self):
        pl.semaphore_wait(pltpu.get_barrier_semaphore(), 9)

    def z_push(self, way, ref, recv, late=0):
        to = (self.mp + (1 if way == 0 else N_MP - 1)) % N_MP
        pltpu.make_async_remote_copy(
            ref, ref, self.zs.at[way, late], recv, device_id={"mp": to}, device_id_type=MESH
        ).start()

    def z_take(self, ref, recv):
        pltpu.make_async_copy(ref, ref, recv).wait()

    def own_part(self, src, chunk, part):
        if part == 2:
            return self.held.at[src, 1, chunk]
        return self.held.at[src, 0, chunk, part * SPILL : (part + 1) * SPILL]

    def z_begin(self, chunk, part):
        for way in (0, 1):
            self.z_push(way, self.own_part(self.mp, chunk, part), self.zf.at[way, chunk, part // 2])

    def behind(self, way, step):
        return (self.mp + (N_MP - step if way == 0 else step)) % N_MP

    def z_first(self, chunk, half):
        for way in (0, 1):
            ref = self.held.at[self.behind(way, 1), half, chunk]
            self.z_take(ref, self.zf.at[way, chunk, half])
            self.z_push(way, ref, self.zr.at[way, 0, 2 * chunk + half])

    def z_ref(self, way, step, piece):
        return self.held.at[self.behind(way, step + 1), piece % 2, piece // 2]

    def z_arrived(self, way, step, piece):
        self.z_take(self.z_ref(way, step, piece), self.zr.at[way, step - 1, piece])

    def relay(self, way, step, pieces):
        late = 1 if step == 3 else 0
        for piece in pieces:
            self.z_arrived(way, step - 1, piece)
            self.z_push(way, self.z_ref(way, step - 1, piece), self.zr.at[way, step - 1, piece], late)

    def w_rows(self, y, x, part):
        at = seq_at(y, x, self.core) * ROWS_W
        size = ROWS_W
        if part is not None:
            size = ROWS_W // 2
            at = at + part * size
        return self.weight.at[pl.ds(pl.multiple_of(at, size), size), :]

    def w_copy(self, send, recv, ref, to):
        return pltpu.make_async_remote_copy(
            ref, ref, send, recv, device_id={"seq": to}, device_id_type=MESH
        )

    def x_copy(self, way, step):
        d = 1 if way == 0 else SIDE - 1
        ref = self.w_rows(self.y, self.x + step * (SIDE - d), None if step == 0 else way)
        return self.w_copy(self.ws, self.xr.at[way, step], ref, seq_at(self.y, self.x + d, self.core))

    def x_arrived(self, way, step):
        d = 1 if way == 0 else SIDE - 1
        ref = self.w_rows(self.y, self.x + (step + 1) * (SIDE - d), None if step == 0 else way)
        self.z_take(ref, self.xr.at[way, step])

    def y_copy(self, way, step, dx):
        d = 1 if way == 0 else SIDE - 1
        ref = self.w_rows(self.y + step * (SIDE - d), self.x + dx, None if step == 0 else way)
        return self.w_copy(
            self.ws, self.yr.at[way, step, dx], ref, seq_at(self.y + d, self.x, self.core)
        )

    def y_arrived(self, way, step, dx):
        d = 1 if way == 0 else SIDE - 1
        ref = self.w_rows(self.y + (step + 1) * (SIDE - d), self.x + dx, None if step == 0 else way)
        self.z_take(ref, self.yr.at[way, step, dx])

    def c_copy(self, dy, dx):
        ref = self.w_rows(self.y + dy, self.x + dx, None)
        return self.w_copy(
            self.ws, self.cr, ref, seq_at(self.y, self.x, 1 - self.core)
        )

    def s_copy(self, way, chunk, ref):
        into = (self.left if way == 0 else self.right).at[chunk]
        to = (self.seq + (1 if way == 0 else 31)) % 32
        return pltpu.make_async_remote_copy(
            ref, into, self.ss, self.sr.at[way, chunk],
            device_id={"seq": to}, device_id_type=MESH,
        )

    def w_begin(self):
        for way in (0, 1):
            self.x_copy(way, 0).start()
            self.y_copy(way, 0, 0).start()
        self.c_copy(0, 0).start()

    def w_row(self):
        for way, dx in ((0, SIDE - 1), (1, 1)):
            self.x_arrived(way, 0)
            self.x_copy(way, 1).start()
            for to in (0, 1):
                self.y_copy(to, 0, dx).start()
            self.c_copy(0, dx).start()

    def w_far(self):
        for way in (0, 1):
            self.x_arrived(way, 1)
        for to in (0, 1):
            self.y_copy(to, 0, 2).start()
        self.c_copy(0, 2).start()

    def w_near(self, dx):
        for way, dy in ((0, SIDE - 1), (1, 1)):
            self.y_arrived(way, 0, dx)
            self.y_copy(way, 1, dx).start()
            self.c_copy(dy, dx).start()

    def w_last(self, dx):
        for way in (0, 1):
            self.y_arrived(way, 1, dx)
        self.c_copy(2, dx).start()

    def w_end(self):
        self.z_take(self.weight.at[0 : SIDE * SIDE * ROWS_W], self.cr)

    def leave(self):
        for way in (0, 1):
            ref = self.held.at[0 : N_MP // 2 - 1]
            self.z_take(ref, self.zs.at[way, 0])
            self.z_take(self.held.at[0, 0], self.zs.at[way, 1])
        sent = (2 + 2 * SIDE) * (ROWS_W + ROWS_W // 2) + SIDE * SIDE * ROWS_W
        self.z_take(self.weight.at[0:sent], self.ws)
        self.z_take(self.held.at[0, 0], self.ss)


COLS_STEP = 256


def part_product(held, weight, src, half, chunks, cols):
    lhs = jnp.concatenate([held[src, half, q] for q in chunks], axis=1)
    rhs = jnp.concatenate(
        [weight[pl.ds(pl.multiple_of((src * CHUNKS + q) * WIDE, WIDE), WIDE), cols] for q in chunks], axis=0
    )
    return jnp.dot(lhs, rhs, preferred_element_type=F32)


def columns(n):
    return pl.ds(pl.multiple_of(n * COLS_STEP, COLS_STEP), COLS_STEP)


def add_product(held, weight, total, src, half, chunks, fresh=False):
    def body(n, _):
        cols = columns(n)
        value = part_product(held, weight, src, half, chunks, cols)
        if fresh:
            total[half, :, cols] = value
        else:
            total[half, :, cols] += value
        return 0

    lax.fori_loop(0, COLS // COLS_STEP, body, 0)


def finish(held, weight, total, out, src, half, chunks):
    def body(n, _):
        cols = columns(n)
        value = (total[half, :, cols] + part_product(held, weight, src, half, chunks, cols)).astype(BF16)
        if half == 0:
            out[SPILL : SPILL + HALF, cols] = value
        else:
            out[0:SPILL, cols] = value[0:SPILL]
            out[TOK - SPILL : TOK, cols] = value[SPILL:]
        return 0

    lax.fori_loop(0, COLS // COLS_STEP, body, 0)


def source_of(mp, u):
    p = u // 2
    far = (p + 1) // 2
    return (mp + N_MP + far * (1 - 2 * (p % 2))) % N_MP


def add_sources(held, weight, total, mp, low, high):
    def body(u, _):
        add_product(held, weight, total, source_of(mp, u), u % 2, range(CHUNKS))
        return 0

    lax.fori_loop(low, high, body, 0)


SEGMENTS = (
    (((2, 6),), ((3, 6),)),
    (((6, 8),), ((6, 8),)),
    (((0, 2), (8, BLOCKS)), ((0, 3), (8, BLOCKS))),
)


def mix_kernel(projections, own_weight, offsets, owners, short_filter, long_filter, skip, out, *scratch):
    panels, masks, later, near, factors, taps, pick, circ, direct, query, product, gated = scratch[:12]
    mine, outgoing, held, weight, total, left, right, in_sem, own_sem = scratch[12:21]
    links = Links(held, weight, left, right, scratch[21:])
    mp = links.mp

    def fetch(q):
        return pltpu.make_async_copy(
            projections.at[:, pl.ds(pl.multiple_of(q * WIDE, WIDE), WIDE), :],
            panels.at[q, :, :, PAD * LONG :],
            in_sem.at[q],
        )

    own = pltpu.make_async_copy(own_weight, links.w_rows(links.y, links.x, None), own_sem)
    links.greet()
    fetch(0).start()
    own.start()
    for q in range(1, CHUNKS):
        fetch(q).start()
    start, coarse, fine, limit = owner_span(links.seq, offsets, owners)
    clear = jnp.zeros((3, WIDE, PAD * LONG), BF16)
    panels[0, :, :, 0 : PAD * LONG] = clear
    prepare(mp, fine, short_filter, long_filter, near, taps, pick, product, gated)
    mark_blocks(start, range(2, 6), offsets, masks, later)
    own.wait()
    for q in range(CHUNKS):
        fetch(q).wait()

    def spill(way, q):
        return links.s_copy(way, q, outgoing.at[q, way])

    def edges(q):
        for way in (0, 1):
            into = (left if way == 0 else right).at[q]
            links.z_take(into, links.sr.at[way, q])
        held[mp, 1, q, 0:SPILL] = mine[q, 0] + left[q]
        held[mp, 1, q, SPILL : 2 * SPILL] = mine[q, 1] + right[q]
        links.z_begin(q, 2)

    def stages(q, segment):
        short_ranges, long_ranges = SEGMENTS[segment]
        short_stage(
            mp, q, short_ranges, segment == 0, coarse, panels, near, factors, skip, later, taps, circ, direct, query, product
        )
        for low, high in long_ranges:
            long_stage(q, low, high, masks, circ, direct, query, product, gated)

    def second(piece):
        for way in (0, 1):
            links.relay(way, 2, (piece,))

    def at_chunk(q, steps):
        for n, step in steps:
            pl.when(q == n)(step)

    def opening(q):
        stages(q, 0)
        held[mp, 0, q, 0:SPILL] = place(limit, q, 2, pick, gated)

    opening(0)
    links.meet()
    links.z_begin(0, 0)
    links.w_begin()
    mark_blocks(start, (6, 7), offsets, masks, later)

    def middle(q, _):
        stages(q, 1)
        held[mp, 0, q, SPILL : 2 * SPILL] = place(limit, q, 3, pick, gated)
        links.z_begin(q, 1)

        @pl.when(q < CHUNKS - 1)
        def _():
            panels[q + 1, :, :, 0 : PAD * LONG] = clear
            opening(q + 1)
            links.z_begin(q + 1, 0)

        at_chunk(
            q,
            (
                (0, lambda: links.z_first(0, 0)),
                (1, links.w_row),
                (2, lambda: links.z_first(1, 0)),
                (3, lambda: links.z_first(2, 0)),
                (3, links.w_far),
                (3, lambda: links.w_near(0)),
            ),
        )
        return 0

    lax.fori_loop(0, CHUNKS, middle, 0)
    mark_blocks(start, (0, 1, 8, 9, 10, 11), offsets, masks, later)

    def outer(q, _):
        stages(q, 2)
        outgoing[q, 0] = place(limit, q, 5, pick, gated)
        outgoing[q, 1] = place(limit, q, 0, pick, gated)
        for way in (0, 1):
            spill(way, q).start()
        mine[q, 0] = place(limit, q, 1, pick, gated)
        mine[q, 1] = place(limit, q, 4, pick, gated)
        @pl.when(q >= 1)
        def _():
            edges(q - 1)

        at_chunk(
            q,
            (
                (0, lambda: second(0)),
                (1, lambda: links.z_first(3, 0)),
                (2, lambda: second(2)),
                (3, lambda: links.z_first(0, 1)),
                (0, lambda: links.w_near(SIDE - 1)),
                (1, lambda: links.w_near(1)),
                (2, lambda: links.w_near(2)),
            ),
        )
        return 0

    lax.fori_loop(0, CHUNKS, outer, 0)
    edges(CHUNKS - 1)
    links.w_last(0)
    links.w_last(SIDE - 1)
    links.z_first(1, 1)
    links.w_last(1)
    links.w_last(2)
    links.w_end()
    for half in (0, 1):
        add_product(held, weight, total, mp, half, range(CHUNKS), True)
    links.z_first(2, 1)
    links.z_first(3, 1)
    second(4)
    second(6)
    add_sources(held, weight, total, mp, 2, 4)
    second(1)
    add_sources(held, weight, total, mp, 4, 6)
    for k in (3, 5, 7):
        second(k)
    add_sources(held, weight, total, mp, 6, 10)
    for half in (0, 1):
        for k in (0, 1):
            links.relay(0, 3, (2 * k + half,))
            links.z_arrived(1, 2, 2 * k + half)
        for k in (2, 3):
            links.relay(1, 3, (2 * k + half,))
            links.z_arrived(0, 2, 2 * k + half)
        for d in (3, N_MP - 3):
            add_product(held, weight, total, (mp + d) % N_MP, half, range(CHUNKS))
    far = (mp + N_MP // 2) % N_MP

    def last(half, k):
        links.z_arrived(0, 3, 2 * k + half)
        links.z_arrived(1, 3, 2 * (k + 2) + half)

    last(0, 0)
    last(0, 1)
    finish(held, weight, total, out, far, 0, range(CHUNKS))
    last(1, 0)
    add_product(held, weight, total, far, 1, (0, 2))
    last(1, 1)
    finish(held, weight, total, out, far, 1, (1, 3))
    links.leave()


FILTER_SCRATCH = [
    pltpu.VMEM((CHUNKS, 3, WIDE, PAD * LONG + CAP), BF16),
    pltpu.VMEM((BLOCKS, 2 * LONG, LONG), BF16),
    pltpu.VMEM((SHORT - 1, 8, CAP), F32),
    pltpu.VMEM((3, WIDE, WIDE), F32),
    pltpu.VMEM((CHUNKS, 3 * SHORT, GROUPS, WIDE), F32),
    pltpu.VMEM((CHUNKS * GROUPS, LONG), F32),
    pltpu.VMEM((SPILL, 3 * LONG), BF16),
    pltpu.VMEM((CHUNKS, GROUPS, LONG, LONG), BF16),
    pltpu.VMEM((CHUNKS, WIDE, WIDE), F32),
    pltpu.VMEM((CHUNKS, WIDE, CAP), BF16),
    pltpu.VMEM((CHUNKS, WIDE, LONG + CAP), BF16),
    pltpu.VMEM((CHUNKS, WIDE, LONG + CAP), BF16),
    pltpu.VMEM((CHUNKS, 2, SPILL, WIDE), BF16),
    pltpu.VMEM((CHUNKS, 2, SPILL, WIDE), BF16),
]
LINK_SCRATCH = [
    pltpu.VMEM((N_MP, 2, CHUNKS, HALF, WIDE), BF16),
    pltpu.VMEM((N_MP * DEPTH, COLS), BF16),
    pltpu.VMEM((2, HALF, COLS), F32),
    pltpu.VMEM((CHUNKS, SPILL, WIDE), BF16),
    pltpu.VMEM((CHUNKS, SPILL, WIDE), BF16),
    pltpu.SemaphoreType.DMA((CHUNKS,)),
    pltpu.SemaphoreType.DMA,
    pltpu.SemaphoreType.DMA((2, 2)),
    pltpu.SemaphoreType.DMA((2, CHUNKS, 2)),
    pltpu.SemaphoreType.DMA((2, 3, PIECES)),
    pltpu.SemaphoreType.DMA,
    pltpu.SemaphoreType.DMA((2, 2)),
    pltpu.SemaphoreType.DMA((2, 2, SIDE)),
    pltpu.SemaphoreType.DMA,
    pltpu.SemaphoreType.DMA,
    pltpu.SemaphoreType.DMA((2, CHUNKS)),
]


def per_device(projections, lengths, owners, offsets, short_filter, long_filter, skip, out_weight):
    vmem = pl.BlockSpec(memory_space=pltpu.VMEM)
    anywhere = pl.BlockSpec(memory_space=pl.ANY)
    return pl.pallas_call(
        mix_kernel,
        out_shape=pltpu.VMEM((TOK, COLS), BF16),
        in_specs=[anywhere, anywhere] + [vmem] * 5,
        out_specs=vmem,
        scratch_shapes=FILTER_SCRATCH + LINK_SCRATCH,
        compiler_params=pltpu.CompilerParams(
            collective_id=0, has_side_effects=True, vmem_limit_bytes=60 * 2**20
        ),
    )(
        projections,
        out_weight,
        offsets.reshape(1, -1),
        owners.reshape(1, -1),
        short_filter.transpose(0, 2, 1),
        long_filter,
        skip.reshape(-1, WIDE),
    )


def solution(mesh):
    placed = (P(None, "mp", "seq"), P(), P(), P(), P(), P(), P(), P("seq", "mp"))
    return jax.shard_map(
        per_device, mesh=mesh, in_specs=placed, out_specs=P("seq", "mp"), check_vma=False
    )
```

```python
import functools

import jax
import jax.numpy as jnp
from jax import lax
from jax.experimental import pallas as pl
from jax.experimental.pallas import tpu as pltpu
from jax.sharding import PartitionSpec as P

MESH = pl.DeviceIdType.MESH
F32 = jnp.float32
BF16 = jnp.bfloat16

GSIZE = 16
SHORT = 7
LONG = 128
TOK = 1024
SPILL = 256
CAP = 1536
TOKENS = 32768
WIDE = 128
CHUNKS = 4
GROUPS = WIDE // GSIZE
BLOCKS = CAP // LONG
PAD = 2 * SPILL // LONG


def iota(shape, dim):
    return lax.broadcasted_iota(jnp.int32, shape, dim)


def owner_span(seq, offsets, owners):
    off = offsets[...]
    own = owners[...]
    first = jnp.min(jnp.where(own == seq, off, TOKENS), axis=1, keepdims=True)
    after = jnp.min(jnp.where(own == seq + 1, off, TOKENS), axis=1, keepdims=True)
    shift = first - seq * TOK + SPILL
    steps = lax.shift_right_arithmetic(shift, 7)
    coarse = steps * LONG
    return first - coarse, steps, shift - coarse, after - first + shift


def mark_blocks(start, blocks, offsets, masks, later, bare=()):
    column = jnp.broadcast_to(offsets[...], (LONG, LONG)).T
    lag = iota((LONG, LONG), 1) - iota((LONG, LONG), 0)
    older = jnp.where(lag < 0, lag + LONG, TOKENS)
    newer = jnp.where(lag >= 0, lag, TOKENS)
    for b in blocks:
        token = start + iota((1, LONG), 1) + b * LONG
        begin = jnp.max(jnp.where(column <= token, column, 0), axis=0, keepdims=True)
        pos = jnp.broadcast_to(token - begin, (8, LONG))
        wide = jnp.broadcast_to(token - begin, (LONG, LONG))
        if b not in bare:
            masks[b, 0:LONG, :] = jnp.where(older <= wide, 1.0, 0.0).astype(BF16)
            masks[b, LONG : 2 * LONG, :] = jnp.where(newer <= wide, 1.0, 0.0).astype(BF16)
        for j in range(1, SHORT):
            later[j - 1, :, b * LONG : (b + 1) * LONG] = jnp.where(pos >= j, 1.0, 0.0)


def prepare(model, fine, short_filter, long_filter, near, taps, pick):
    rows = CHUNKS * GROUPS
    taps[...] = long_filter[pl.ds(pl.multiple_of(model * rows, rows), rows), :].astype(F32)
    aside = pl.ds(pl.multiple_of(model // 4 * WIDE, WIDE), WIDE)
    for p in range(3):
        block = jnp.concatenate([short_filter[p, :, aside], jnp.zeros((WIDE - SHORT, WIDE), F32)], axis=0)
        near[p] = block.T
    turned = iota((SPILL, 3 * LONG), 1) - iota((SPILL, 3 * LONG), 0) - LONG
    pick[...] = jnp.where(turned == -fine, 1.0, 0.0).astype(BF16)


def short_stage(model, chunk, ranges, fresh, coarse, panels, near, factors, skip, later, taps, circ, direct, query, product):
    if fresh:
        gains = skip[pl.ds(model * CHUNKS + chunk, 1), :]
        direct[chunk] = jnp.broadcast_to(gains, (WIDE, WIDE)).T
        first_row = pl.multiple_of(model % 4 * (CHUNKS * GROUPS) + chunk * GROUPS, GROUPS)
        for p in range(3):
            mine = near[p, pl.ds(first_row, GROUPS), :]
            for j in range(SHORT):
                factors[chunk, p * SHORT + j] = jnp.broadcast_to(mine[:, j : j + 1], (GROUPS, WIDE))
    lane = iota((GSIZE, LONG), 1)
    steps = jnp.broadcast_to(coarse, (GSIZE, LONG))

    def short(g, _):
        ch = pl.ds(pl.multiple_of(g * GSIZE, GSIZE), GSIZE)
        row = chunk * GROUPS + g

        def cells(p, b):
            x = panels[chunk, p, ch, (b + PAD) * LONG : (b + PAD + 1) * LONG]
            for k in range(1, PAD + 1):
                at = (b + PAD - k) * LONG
                x = jnp.where(steps == k, panels[chunk, p, ch, at : at + LONG], x)
            return x

        if fresh:
            line = jnp.broadcast_to(taps[pl.ds(row, 1), :], (LONG, LONG))
            circ[chunk, g] = pltpu.roll(line, 0, 1, stride=1, stride_axis=0).astype(BF16)
        factor = [
            [jnp.broadcast_to(factors[chunk, p * SHORT + j, pl.ds(g, 1), :], (8, LONG)) for j in range(SHORT)]
            for p in range(3)
        ]
        for low_block, high_block in ranges:
            rolled = [[None] * SHORT for _ in range(3)]
            if low_block > 0:
                before = [cells(p, low_block - 1) for p in range(3)]
                rolled = [[pltpu.roll(before[p], j, 1) for j in range(SHORT)] for p in range(3)]
            for b in range(low_block, high_block):
                at = slice(b * LONG, (b + 1) * LONG)
                sums = []
                for p in range(3):
                    x = cells(p, b)
                    wide = x.astype(F32)
                    low = factor[p][0] * wide[0:8]
                    high = factor[p][0] * wide[8:16]
                    for j in range(1, SHORT):
                        turned = pltpu.roll(x, j, 1)
                        before = rolled[p][j]
                        rolled[p][j] = turned
                        if b > 0:
                            turned = jnp.where(lane < j, before, turned)
                        weight = factor[p][j] * later[j - 1, :, at]
                        wide = turned.astype(F32)
                        low = low + weight * wide[0:8]
                        high = high + weight * wide[8:16]
                    sums.append(jnp.concatenate([low, high], axis=0))
                query[chunk, ch, at] = sums[0].astype(BF16)
                product[chunk, ch, (b + 1) * LONG : (b + 2) * LONG] = (sums[1] * sums[2]).astype(BF16)
        return 0

    lax.fori_loop(0, GROUPS, short, 0)


def long_stage(chunk, low_block, high_block, masks, circ, direct, query, product, gated):
    def long(b, _):
        at = pl.multiple_of(b * LONG, LONG)
        older = masks[b, 0:LONG, :]
        newer = masks[b, LONG : 2 * LONG, :]
        for g in range(GROUPS):
            ch = slice(g * GSIZE, (g + 1) * GSIZE)
            matrix = jnp.concatenate([circ[chunk, g] * older, circ[chunk, g] * newer], axis=0)
            window = product[chunk, ch, pl.ds(at, 2 * LONG)]
            w = jnp.dot(window, matrix, preferred_element_type=F32)
            now = product[chunk, ch, pl.ds(at + LONG, LONG)].astype(F32)
            w = w + direct[chunk, ch, :] * now
            out = query[chunk, ch, pl.ds(at, LONG)].astype(F32) * w
            gated[chunk, ch, pl.ds(at + LONG, LONG)] = out.astype(BF16)
        return 0

    lax.fori_loop(low_block, high_block, long, 0)


def place(limit, chunk, k, pick, gated):
    at = k * SPILL
    if not isinstance(k, int):
        at = pl.multiple_of(at, SPILL)
    block = gated[chunk, :, pl.ds(at, 3 * LONG)]
    moved = lax.dot_general(
        pick[...], block, (((1,), (1,)), ((), ())), preferred_element_type=F32
    )
    mine = iota((SPILL, WIDE), 0) + k * SPILL < limit
    return jnp.where(mine, moved, 0.0).astype(BF16)


N_MP = 8
SIDE = 4
DEPTH = 4 * WIDE
COLS = 1024
ROWS_W = WIDE
HALF = TOK // 2
PIECES = 2 * CHUNKS


def position():
    seq = lax.axis_index("seq")
    return seq, lax.axis_index("mp"), seq // 8, (seq // 2) % SIDE, seq % 2


def seq_at(y, x, core):
    return ((y % SIDE) * SIDE + x % SIDE) * 2 + core


class Links:
    def __init__(self, held, weight, left, right, sems):
        self.held, self.weight, self.left, self.right = held, weight, left, right
        (self.zs, self.zf, self.zr, self.ws, self.xr, self.yr, self.cr, self.ss, self.sr) = sems
        self.seq, self.mp, self.y, self.x, self.core = position()

    def greet(self):
        barrier = pltpu.get_barrier_semaphore()
        targets = [{"mp": (self.mp + d) % N_MP} for d in (1, N_MP - 1)]
        targets += [{"seq": (self.seq + d) % 32} for d in (1, 31)]
        targets += [{"seq": seq_at(self.y, self.x + d, self.core)} for d in (1, SIDE - 1)]
        targets += [{"seq": seq_at(self.y + d, self.x, self.core)} for d in (1, SIDE - 1)]
        targets += [{"seq": seq_at(self.y, self.x, 1 - self.core)}]
        for target in targets:
            pl.semaphore_signal(barrier, inc=1, device_id=target, device_id_type=MESH)

    def meet(self):
        pl.semaphore_wait(pltpu.get_barrier_semaphore(), 9)

    def z_push(self, way, ref, recv, late=0):
        to = (self.mp + (1 if way == 0 else N_MP - 1)) % N_MP
        pltpu.make_async_remote_copy(
            ref, ref, self.zs.at[way, late], recv, device_id={"mp": to}, device_id_type=MESH
        ).start()

    def z_take(self, ref, recv):
        pltpu.make_async_copy(ref, ref, recv).wait()

    def own_part(self, src, chunk, part):
        if part == 2:
            return self.held.at[src, 1, chunk]
        return self.held.at[src, 0, chunk, part * SPILL : (part + 1) * SPILL]

    def z_begin(self, chunk, part):
        slot = part // 2
        if part == 1:
            slot = (CHUNKS - chunk) // CHUNKS * 2
        for way in (0, 1):
            self.z_push(way, self.own_part(self.mp, chunk, part), self.zf.at[way, chunk, slot])

    def behind(self, way, step):
        return (self.mp + (N_MP - step if way == 0 else step)) % N_MP

    def z_first(self, chunk, half):
        for way in (0, 1):
            ref = self.held.at[self.behind(way, 1), half, chunk]
            self.z_take(ref, self.zf.at[way, chunk, half])
            self.z_push(way, ref, self.zr.at[way, 0, 2 * chunk + half])

    def z_half(self, part):
        for way in (0, 1):
            ref = self.own_part(self.behind(way, 1), 0, part)
            self.z_take(ref, self.zf.at[way, 0, 2 * part])
            self.z_push(way, ref, self.zr.at[way, 0, 0])

    def z_ref(self, way, step, piece):
        return self.held.at[self.behind(way, step + 1), piece % 2, piece // 2]

    def z_arrived(self, way, step, piece):
        self.z_take(self.z_ref(way, step, piece), self.zr.at[way, step - 1, piece])

    def relay(self, way, step, pieces):
        late = 1 if step == 3 else 0
        for piece in pieces:
            self.z_arrived(way, step - 1, piece)
            self.z_push(way, self.z_ref(way, step - 1, piece), self.zr.at[way, step - 1, piece], late)

    def w_rows(self, y, x, part):
        at = seq_at(y, x, self.core) * ROWS_W
        size = ROWS_W
        if part is not None:
            size = ROWS_W // 2
            at = at + part * size
        return self.weight.at[pl.ds(pl.multiple_of(at, size), size), :]

    def w_copy(self, send, recv, ref, to):
        return pltpu.make_async_remote_copy(
            ref, ref, send, recv, device_id={"seq": to}, device_id_type=MESH
        )

    def x_copy(self, way, step):
        d = 1 if way == 0 else SIDE - 1
        ref = self.w_rows(self.y, self.x + step * (SIDE - d), None if step == 0 else way)
        return self.w_copy(self.ws, self.xr.at[way, step], ref, seq_at(self.y, self.x + d, self.core))

    def x_arrived(self, way, step):
        d = 1 if way == 0 else SIDE - 1
        ref = self.w_rows(self.y, self.x + (step + 1) * (SIDE - d), None if step == 0 else way)
        self.z_take(ref, self.xr.at[way, step])

    def y_copy(self, way, step, dx):
        d = 1 if way == 0 else SIDE - 1
        ref = self.w_rows(self.y + step * (SIDE - d), self.x + dx, None if step == 0 else way)
        return self.w_copy(
            self.ws, self.yr.at[way, step, dx], ref, seq_at(self.y + d, self.x, self.core)
        )

    def y_arrived(self, way, step, dx):
        d = 1 if way == 0 else SIDE - 1
        ref = self.w_rows(self.y + (step + 1) * (SIDE - d), self.x + dx, None if step == 0 else way)
        self.z_take(ref, self.yr.at[way, step, dx])

    def c_copy(self, dy, dx):
        ref = self.w_rows(self.y + dy, self.x + dx, None)
        return self.w_copy(
            self.ws, self.cr, ref, seq_at(self.y, self.x, 1 - self.core)
        )

    def s_copy(self, way, chunk, ref):
        into = (self.left if way == 0 else self.right).at[chunk]
        to = (self.seq + (1 if way == 0 else 31)) % 32
        return pltpu.make_async_remote_copy(
            ref, into, self.ss, self.sr.at[way, chunk],
            device_id={"seq": to}, device_id_type=MESH,
        )

    def w_begin(self):
        for way in (0, 1):
            self.x_copy(way, 0).start()
            self.y_copy(way, 0, 0).start()
        self.c_copy(0, 0).start()

    def w_row(self):
        for way, dx in ((0, SIDE - 1), (1, 1)):
            self.x_arrived(way, 0)
            self.x_copy(way, 1).start()
            for to in (0, 1):
                self.y_copy(to, 0, dx).start()
            self.c_copy(0, dx).start()

    def w_far(self):
        for way in (0, 1):
            self.x_arrived(way, 1)
        for to in (0, 1):
            self.y_copy(to, 0, 2).start()
        self.c_copy(0, 2).start()

    def w_near(self, dx):
        for way, dy in ((0, SIDE - 1), (1, 1)):
            self.y_arrived(way, 0, dx)
            self.y_copy(way, 1, dx).start()
            self.c_copy(dy, dx).start()

    def w_last(self, dx):
        for way in (0, 1):
            self.y_arrived(way, 1, dx)
        self.c_copy(2, dx).start()

    def w_end(self):
        self.z_take(self.weight.at[0 : SIDE * SIDE * ROWS_W], self.cr)

    def leave(self):
        for way in (0, 1):
            ref = self.held.at[0 : N_MP // 2 - 1]
            self.z_take(ref, self.zs.at[way, 0])
            self.z_take(self.held.at[0, 0], self.zs.at[way, 1])
        sent = (2 + 2 * SIDE) * (ROWS_W + ROWS_W // 2) + SIDE * SIDE * ROWS_W
        self.z_take(self.weight.at[0:sent], self.ws)
        self.z_take(self.held.at[0, 0], self.ss)


COLS_STEP = 256


def part_product(held, weight, src, half, chunks, cols):
    lhs = jnp.concatenate([held[src, half, q] for q in chunks], axis=1)
    rhs = jnp.concatenate(
        [weight[pl.ds(pl.multiple_of((src * CHUNKS + q) * WIDE, WIDE), WIDE), cols] for q in chunks], axis=0
    )
    return jnp.dot(lhs, rhs, preferred_element_type=F32)


def columns(n):
    return pl.ds(pl.multiple_of(n * COLS_STEP, COLS_STEP), COLS_STEP)


def add_product(held, weight, total, src, half, chunks, fresh=False):
    def body(n, _):
        cols = columns(n)
        value = part_product(held, weight, src, half, chunks, cols)
        if fresh:
            total[half, :, cols] = value
        else:
            total[half, :, cols] += value
        return 0

    lax.fori_loop(0, COLS // COLS_STEP, body, 0)


def finish(held, weight, total, out, src, half, chunks):
    def body(n, _):
        cols = columns(n)
        value = (total[half, :, cols] + part_product(held, weight, src, half, chunks, cols)).astype(BF16)
        if half == 0:
            out[SPILL : SPILL + HALF, cols] = value
        else:
            out[0:SPILL, cols] = value[0:SPILL]
            out[TOK - SPILL : TOK, cols] = value[SPILL:]
        return 0

    lax.fori_loop(0, COLS // COLS_STEP, body, 0)


def source_of(mp, u):
    p = u // 2
    far = (p + 1) // 2
    return (mp + N_MP + far * (1 - 2 * (p % 2))) % N_MP


def add_sources(held, weight, total, mp, low, high):
    def body(u, _):
        add_product(held, weight, total, source_of(mp, u), u % 2, range(CHUNKS))
        return 0

    lax.fori_loop(low, high, body, 0)


SEGMENTS = (
    (((2, 6),), ((3, 6),)),
    (((6, 8),), ((6, 8),)),
    (((0, 2), (8, BLOCKS)), ((0, 3), (8, BLOCKS))),
)


def mix_kernel(projections, own_weight, offsets, owners, short_filter, long_filter, skip, out, *scratch):
    panels, masks, later, near, factors, taps, pick, circ, direct, query, product, gated = scratch[:12]
    mine, outgoing, held, weight, total, left, right, in_sem, own_sem = scratch[12:21]
    links = Links(held, weight, left, right, scratch[21:])
    mp = links.mp

    def fetch(q):
        return pltpu.make_async_copy(
            projections.at[:, pl.ds(pl.multiple_of(q * WIDE, WIDE), WIDE), :],
            panels.at[q, :, :, PAD * LONG :],
            in_sem.at[q],
        )

    own = pltpu.make_async_copy(own_weight, links.w_rows(links.y, links.x, None), own_sem)
    links.greet()
    fetch(0).start()
    own.start()
    for q in range(1, CHUNKS):
        fetch(q).start()
    start, coarse, fine, limit = owner_span(links.seq, offsets, owners)
    clear = jnp.zeros((3, WIDE, PAD * LONG), BF16)
    panels[0, :, :, LONG : PAD * LONG] = clear[:, :, LONG:]
    prepare(mp, fine, short_filter, long_filter, near, taps, pick)
    mark_blocks(start, range(2, 6), offsets, masks, later, (2,))
    own.wait()
    fetch(0).wait()

    def spill(way, q):
        return links.s_copy(way, q, outgoing.at[q, way])

    def edges(q):
        for way in (0, 1):
            into = (left if way == 0 else right).at[q]
            links.z_take(into, links.sr.at[way, q])
        held[mp, 1, q, 0:SPILL] = mine[q, 0] + left[q]
        held[mp, 1, q, SPILL : 2 * SPILL] = mine[q, 1] + right[q]
        links.z_begin(q, 2)

    def stages(q, segment, between=None):
        short_ranges, long_ranges = SEGMENTS[segment]
        short_stage(
            mp, q, short_ranges, segment == 0, coarse, panels, near, factors, skip, later, taps, circ, direct, query, product
        )
        if between is not None:
            between()
        for low, high in long_ranges:
            long_stage(q, low, high, masks, circ, direct, query, product, gated)

    def second(piece):
        for way in (0, 1):
            links.relay(way, 2, (piece,))

    def at_chunk(q, steps):
        for n, step in steps:
            pl.when(q == n)(step)

    def opening(q, between=None):
        stages(q, 0, between)
        held[mp, 0, q, 0:SPILL] = place(limit, q, 2, pick, gated)

    opening(0)
    links.meet()
    links.z_begin(0, 0)
    links.w_begin()
    panels[0, :, :, 0:LONG] = clear[:, :, 0:LONG]
    product[:, :, 0:LONG] = jnp.zeros((CHUNKS, WIDE, LONG), BF16)
    gated[:, :, 0:LONG] = jnp.zeros((CHUNKS, WIDE, LONG), BF16)
    mark_blocks(start, (6, 7), offsets, masks, later)

    def middle(q, _):
        stages(q, 1)
        held[mp, 0, q, SPILL : 2 * SPILL] = place(limit, q, 3, pick, gated)
        links.z_begin(q, 1)

        @pl.when(q < CHUNKS - 1)
        def _():
            panels[q + 1, :, :, 0 : PAD * LONG] = clear
            fetch(q + 1).wait()
            opening(q + 1, lambda: pl.when(q == 0)(lambda: links.z_half(0)))
            links.z_begin(q + 1, 0)

        at_chunk(
            q,
            (
                (0, lambda: links.z_half(1)),
                (1, links.w_row),
                (2, lambda: links.z_first(1, 0)),
                (3, lambda: links.z_first(2, 0)),
                (3, links.w_far),
                (3, lambda: links.w_near(0)),
            ),
        )
        return 0

    lax.fori_loop(0, CHUNKS, middle, 0)
    mark_blocks(start, (0, 1, 2, 8, 9, 10, 11), offsets, masks, later)

    def outer(q, _):
        stages(q, 2)
        outgoing[q, 0] = place(limit, q, 5, pick, gated)
        outgoing[q, 1] = place(limit, q, 0, pick, gated)
        for way in (0, 1):
            spill(way, q).start()
        mine[q, 0] = place(limit, q, 1, pick, gated)
        mine[q, 1] = place(limit, q, 4, pick, gated)
        @pl.when(q >= 1)
        def _():
            edges(q - 1)

        at_chunk(
            q,
            (
                (0, lambda: second(0)),
                (1, lambda: links.z_first(3, 0)),
                (2, lambda: second(2)),
                (3, lambda: links.z_first(0, 1)),
                (0, lambda: links.w_near(SIDE - 1)),
                (1, lambda: links.w_near(1)),
                (2, lambda: links.w_near(2)),
            ),
        )
        return 0

    lax.fori_loop(0, CHUNKS, outer, 0)
    edges(CHUNKS - 1)
    links.w_last(0)
    links.w_last(SIDE - 1)
    links.z_first(1, 1)
    links.w_last(1)
    links.w_last(2)
    links.w_end()
    for half in (0, 1):
        add_product(held, weight, total, mp, half, range(CHUNKS), True)
    links.z_first(2, 1)
    links.z_first(3, 1)
    second(4)
    second(6)
    add_sources(held, weight, total, mp, 2, 4)
    second(1)
    add_sources(held, weight, total, mp, 4, 6)
    for k in (3, 5, 7):
        second(k)
    add_sources(held, weight, total, mp, 6, 10)
    for half in (0, 1):
        for k in (0, 1):
            links.relay(0, 3, (2 * k + half,))
            links.z_arrived(1, 2, 2 * k + half)
        for k in (2, 3):
            links.relay(1, 3, (2 * k + half,))
            links.z_arrived(0, 2, 2 * k + half)
        for d in (3, N_MP - 3):
            add_product(held, weight, total, (mp + d) % N_MP, half, range(CHUNKS))
    far = (mp + N_MP // 2) % N_MP

    def last(half, k):
        links.z_arrived(0, 3, 2 * k + half)
        links.z_arrived(1, 3, 2 * (k + 2) + half)

    last(0, 0)
    last(0, 1)
    finish(held, weight, total, out, far, 0, range(CHUNKS))
    last(1, 0)
    add_product(held, weight, total, far, 1, (0, 2))
    last(1, 1)
    finish(held, weight, total, out, far, 1, (1, 3))
    links.leave()


FILTER_SCRATCH = [
    pltpu.VMEM((CHUNKS, 3, WIDE, PAD * LONG + CAP), BF16),
    pltpu.VMEM((BLOCKS, 2 * LONG, LONG), BF16),
    pltpu.VMEM((SHORT - 1, 8, CAP), F32),
    pltpu.VMEM((3, WIDE, WIDE), F32),
    pltpu.VMEM((CHUNKS, 3 * SHORT, GROUPS, WIDE), F32),
    pltpu.VMEM((CHUNKS * GROUPS, LONG), F32),
    pltpu.VMEM((SPILL, 3 * LONG), BF16),
    pltpu.VMEM((CHUNKS, GROUPS, LONG, LONG), BF16),
    pltpu.VMEM((CHUNKS, WIDE, WIDE), F32),
    pltpu.VMEM((CHUNKS, WIDE, CAP), BF16),
    pltpu.VMEM((CHUNKS, WIDE, LONG + CAP), BF16),
    pltpu.VMEM((CHUNKS, WIDE, LONG + CAP), BF16),
    pltpu.VMEM((CHUNKS, 2, SPILL, WIDE), BF16),
    pltpu.VMEM((CHUNKS, 2, SPILL, WIDE), BF16),
]
LINK_SCRATCH = [
    pltpu.VMEM((N_MP, 2, CHUNKS, HALF, WIDE), BF16),
    pltpu.VMEM((N_MP * DEPTH, COLS), BF16),
    pltpu.VMEM((2, HALF, COLS), F32),
    pltpu.VMEM((CHUNKS, SPILL, WIDE), BF16),
    pltpu.VMEM((CHUNKS, SPILL, WIDE), BF16),
    pltpu.SemaphoreType.DMA((CHUNKS,)),
    pltpu.SemaphoreType.DMA,
    pltpu.SemaphoreType.DMA((2, 2)),
    pltpu.SemaphoreType.DMA((2, CHUNKS, 3)),
    pltpu.SemaphoreType.DMA((2, 3, PIECES)),
    pltpu.SemaphoreType.DMA,
    pltpu.SemaphoreType.DMA((2, 2)),
    pltpu.SemaphoreType.DMA((2, 2, SIDE)),
    pltpu.SemaphoreType.DMA,
    pltpu.SemaphoreType.DMA,
    pltpu.SemaphoreType.DMA((2, CHUNKS)),
]


def per_device(projections, lengths, owners, offsets, short_filter, long_filter, skip, out_weight):
    vmem = pl.BlockSpec(memory_space=pltpu.VMEM)
    anywhere = pl.BlockSpec(memory_space=pl.ANY)
    return pl.pallas_call(
        mix_kernel,
        out_shape=pltpu.VMEM((TOK, COLS), BF16),
        in_specs=[anywhere, anywhere] + [vmem] * 5,
        out_specs=vmem,
        scratch_shapes=FILTER_SCRATCH + LINK_SCRATCH,
        compiler_params=pltpu.CompilerParams(
            collective_id=0, has_side_effects=True, vmem_limit_bytes=60 * 2**20
        ),
    )(
        projections,
        out_weight,
        offsets.reshape(1, -1),
        owners.reshape(1, -1),
        short_filter.transpose(0, 2, 1),
        long_filter,
        skip.reshape(-1, WIDE),
    )


def solution(mesh):
    placed = (P(None, "mp", "seq"), P(), P(), P(), P(), P(), P(), P("seq", "mp"))
    return jax.shard_map(
        per_device, mesh=mesh, in_specs=placed, out_specs=P("seq", "mp"), check_vma=False
    )
```

```python
import functools

import jax
import jax.numpy as jnp
from jax import lax
from jax.experimental import pallas as pl
from jax.experimental.pallas import tpu as pltpu
from jax.sharding import PartitionSpec as P

MESH = pl.DeviceIdType.MESH
F32 = jnp.float32
BF16 = jnp.bfloat16

GSIZE = 16
SHORT = 7
LONG = 128
TOK = 1024
SPILL = 256
CAP = 1536
TOKENS = 32768
WIDE = 128
CHUNKS = 4
GROUPS = WIDE // GSIZE
BLOCKS = CAP // LONG
PAD = 2 * SPILL // LONG


def iota(shape, dim):
    return lax.broadcasted_iota(jnp.int32, shape, dim)


def owner_span(seq, offsets, owners):
    off = offsets[...]
    own = owners[...]
    first = jnp.min(jnp.where(own == seq, off, TOKENS), axis=1, keepdims=True)
    after = jnp.min(jnp.where(own == seq + 1, off, TOKENS), axis=1, keepdims=True)
    shift = first - seq * TOK + SPILL
    steps = lax.shift_right_arithmetic(shift, 7)
    coarse = steps * LONG
    return first - coarse, steps, shift - coarse, after - first + shift


def mark_blocks(start, blocks, offsets, masks, later, bare=()):
    column = jnp.broadcast_to(offsets[...], (LONG, LONG)).T
    lag = iota((LONG, LONG), 1) - iota((LONG, LONG), 0)
    older = jnp.where(lag < 0, lag + LONG, TOKENS)
    newer = jnp.where(lag >= 0, lag, TOKENS)
    for b in blocks:
        token = start + iota((1, LONG), 1) + b * LONG
        begin = jnp.max(jnp.where(column <= token, column, 0), axis=0, keepdims=True)
        pos = jnp.broadcast_to(token - begin, (8, LONG))
        wide = jnp.broadcast_to(token - begin, (LONG, LONG))
        if b not in bare:
            masks[b, 0:LONG, :] = jnp.where(older <= wide, 1.0, 0.0).astype(BF16)
            masks[b, LONG : 2 * LONG, :] = jnp.where(newer <= wide, 1.0, 0.0).astype(BF16)
        for j in range(1, SHORT):
            later[j - 1, :, b * LONG : (b + 1) * LONG] = jnp.where(pos >= j, 1.0, 0.0)


def prepare(model, fine, short_filter, long_filter, near, taps, pick):
    rows = CHUNKS * GROUPS
    taps[...] = long_filter[pl.ds(pl.multiple_of(model * rows, rows), rows), :].astype(F32)
    aside = pl.ds(pl.multiple_of(model // 4 * WIDE, WIDE), WIDE)
    for p in range(3):
        block = jnp.concatenate([short_filter[p, :, aside], jnp.zeros((WIDE - SHORT, WIDE), F32)], axis=0)
        near[p] = block.T
    turned = iota((SPILL, 3 * LONG), 1) - iota((SPILL, 3 * LONG), 0) - LONG
    pick[...] = jnp.where(turned == -fine, 1.0, 0.0).astype(BF16)


def short_stage(model, chunk, ranges, fresh, coarse, panels, near, factors, skip, later, taps, circ, direct, query, product):
    if fresh:
        gains = skip[pl.ds(model * CHUNKS + chunk, 1), :]
        direct[chunk] = jnp.broadcast_to(gains, (WIDE, WIDE)).T
        first_row = pl.multiple_of(model % 4 * (CHUNKS * GROUPS) + chunk * GROUPS, GROUPS)
        for p in range(3):
            mine = near[p, pl.ds(first_row, GROUPS), :]
            for j in range(SHORT):
                factors[chunk, p * SHORT + j] = jnp.broadcast_to(mine[:, j : j + 1], (GROUPS, WIDE))
    lane = iota((GSIZE, LONG), 1)
    steps = jnp.broadcast_to(coarse, (GSIZE, LONG))

    def short(g, _):
        ch = pl.ds(pl.multiple_of(g * GSIZE, GSIZE), GSIZE)
        row = chunk * GROUPS + g

        def cells(p, b):
            x = panels[chunk, p, ch, (b + PAD) * LONG : (b + PAD + 1) * LONG]
            for k in range(1, PAD + 1):
                at = (b + PAD - k) * LONG
                x = jnp.where(steps == k, panels[chunk, p, ch, at : at + LONG], x)
            return x

        if fresh:
            line = jnp.broadcast_to(taps[pl.ds(row, 1), :], (LONG, LONG))
            circ[chunk, g] = pltpu.roll(line, 0, 1, stride=1, stride_axis=0).astype(BF16)
        factor = [
            [jnp.broadcast_to(factors[chunk, p * SHORT + j, pl.ds(g, 1), :], (8, LONG)) for j in range(SHORT)]
            for p in range(3)
        ]
        for low_block, high_block in ranges:
            rolled = [[None] * SHORT for _ in range(3)]
            if low_block > 0:
                before = [cells(p, low_block - 1) for p in range(3)]
                rolled = [[pltpu.roll(before[p], j, 1) for j in range(SHORT)] for p in range(3)]
            for b in range(low_block, high_block):
                at = slice(b * LONG, (b + 1) * LONG)
                sums = []
                for p in range(3):
                    x = cells(p, b)
                    wide = x.astype(F32)
                    low = factor[p][0] * wide[0:8]
                    high = factor[p][0] * wide[8:16]
                    for j in range(1, SHORT):
                        turned = pltpu.roll(x, j, 1)
                        before = rolled[p][j]
                        rolled[p][j] = turned
                        if b > 0:
                            turned = jnp.where(lane < j, before, turned)
                        weight = factor[p][j] * later[j - 1, :, at]
                        wide = turned.astype(F32)
                        low = low + weight * wide[0:8]
                        high = high + weight * wide[8:16]
                    sums.append(jnp.concatenate([low, high], axis=0))
                query[chunk, ch, at] = sums[0].astype(BF16)
                product[chunk, ch, (b + 1) * LONG : (b + 2) * LONG] = (sums[1] * sums[2]).astype(BF16)
        return 0

    lax.fori_loop(0, GROUPS, short, 0)


def long_stage(chunk, low_block, high_block, masks, circ, direct, query, product, gated):
    def long(b, _):
        at = pl.multiple_of(b * LONG, LONG)
        older = masks[b, 0:LONG, :]
        newer = masks[b, LONG : 2 * LONG, :]
        for g in range(GROUPS):
            ch = slice(g * GSIZE, (g + 1) * GSIZE)
            matrix = jnp.concatenate([circ[chunk, g] * older, circ[chunk, g] * newer], axis=0)
            window = product[chunk, ch, pl.ds(at, 2 * LONG)]
            w = jnp.dot(window, matrix, preferred_element_type=F32)
            now = product[chunk, ch, pl.ds(at + LONG, LONG)].astype(F32)
            w = w + direct[chunk, ch, :] * now
            out = query[chunk, ch, pl.ds(at, LONG)].astype(F32) * w
            gated[chunk, ch, pl.ds(at + LONG, LONG)] = out.astype(BF16)
        return 0

    lax.fori_loop(low_block, high_block, long, 0)


def place(limit, chunk, k, pick, gated):
    at = k * SPILL
    if not isinstance(k, int):
        at = pl.multiple_of(at, SPILL)
    block = gated[chunk, :, pl.ds(at, 3 * LONG)]
    moved = lax.dot_general(
        pick[...], block, (((1,), (1,)), ((), ())), preferred_element_type=F32
    )
    mine = iota((SPILL, WIDE), 0) + k * SPILL < limit
    return jnp.where(mine, moved, 0.0).astype(BF16)


N_MP = 8
SIDE = 4
DEPTH = 4 * WIDE
COLS = 1024
ROWS_W = WIDE
HALF = TOK // 2
PIECES = 2 * CHUNKS


def position():
    seq = lax.axis_index("seq")
    return seq, lax.axis_index("mp"), seq // 8, (seq // 2) % SIDE, seq % 2


def seq_at(y, x, core):
    return ((y % SIDE) * SIDE + x % SIDE) * 2 + core


class Links:
    def __init__(self, held, weight, left, right, sems):
        self.held, self.weight, self.left, self.right = held, weight, left, right
        (self.zs, self.zf, self.zr, self.ws, self.xr, self.yr, self.cr, self.ss, self.sr) = sems
        self.seq, self.mp, self.y, self.x, self.core = position()

    def greet(self):
        barrier = pltpu.get_barrier_semaphore()
        targets = [{"mp": (self.mp + d) % N_MP} for d in (1, N_MP - 1)]
        targets += [{"seq": (self.seq + d) % 32} for d in (1, 31)]
        targets += [{"seq": seq_at(self.y, self.x + d, self.core)} for d in (1, SIDE - 1)]
        targets += [{"seq": seq_at(self.y + d, self.x, self.core)} for d in (1, SIDE - 1)]
        targets += [{"seq": seq_at(self.y, self.x, 1 - self.core)}]
        for target in targets:
            pl.semaphore_signal(barrier, inc=1, device_id=target, device_id_type=MESH)

    def meet(self):
        pl.semaphore_wait(pltpu.get_barrier_semaphore(), 9)

    def z_push(self, way, ref, recv, late=0):
        to = (self.mp + (1 if way == 0 else N_MP - 1)) % N_MP
        pltpu.make_async_remote_copy(
            ref, ref, self.zs.at[way, late], recv, device_id={"mp": to}, device_id_type=MESH
        ).start()

    def z_take(self, ref, recv):
        pltpu.make_async_copy(ref, ref, recv).wait()

    def own_part(self, src, chunk, part):
        if part == 2:
            return self.held.at[src, 1, chunk]
        return self.held.at[src, 0, chunk, part * SPILL : (part + 1) * SPILL]

    def z_begin(self, chunk, part):
        slot = part // 2
        if part == 1:
            slot = (CHUNKS - chunk) // CHUNKS * 2
        for way in (0, 1):
            self.z_push(way, self.own_part(self.mp, chunk, part), self.zf.at[way, chunk, slot])

    def behind(self, way, step):
        return (self.mp + (N_MP - step if way == 0 else step)) % N_MP

    def z_first(self, chunk, half):
        for way in (0, 1):
            ref = self.held.at[self.behind(way, 1), half, chunk]
            self.z_take(ref, self.zf.at[way, chunk, half])
            self.z_push(way, ref, self.zr.at[way, 0, 2 * chunk + half])

    def z_half(self, part):
        for way in (0, 1):
            ref = self.own_part(self.behind(way, 1), 0, part)
            self.z_take(ref, self.zf.at[way, 0, 2 * part])
            self.z_push(way, ref, self.zr.at[way, 0, 0])

    def z_ref(self, way, step, piece):
        return self.held.at[self.behind(way, step + 1), piece % 2, piece // 2]

    def z_arrived(self, way, step, piece):
        self.z_take(self.z_ref(way, step, piece), self.zr.at[way, step - 1, piece])

    def relay(self, way, step, pieces):
        late = 1 if step == 3 else 0
        for piece in pieces:
            self.z_arrived(way, step - 1, piece)
            self.z_push(way, self.z_ref(way, step - 1, piece), self.zr.at[way, step - 1, piece], late)

    def relay_last(self, way, piece):
        self.z_arrived(way, 2, piece)
        for part in (0, 1):
            ref = self.z_ref(way, 2, piece).at[part * SPILL : (part + 1) * SPILL]
            self.z_push(way, ref, self.zr.at[way, 2, (piece + part * CHUNKS) % PIECES], 1)

    def last_arrived(self, way, piece, part):
        ref = self.z_ref(way, 3, piece).at[part * SPILL : (part + 1) * SPILL]
        self.z_take(ref, self.zr.at[way, 2, (piece + part * CHUNKS) % PIECES])

    def w_rows(self, y, x, part):
        at = seq_at(y, x, self.core) * ROWS_W
        size = ROWS_W
        if part is not None:
            size = ROWS_W // 2
            at = at + part * size
        return self.weight.at[pl.ds(pl.multiple_of(at, size), size), :]

    def w_copy(self, send, recv, ref, to):
        return pltpu.make_async_remote_copy(
            ref, ref, send, recv, device_id={"seq": to}, device_id_type=MESH
        )

    def x_copy(self, way, step):
        d = 1 if way == 0 else SIDE - 1
        ref = self.w_rows(self.y, self.x + step * (SIDE - d), None if step == 0 else way)
        return self.w_copy(self.ws, self.xr.at[way, step], ref, seq_at(self.y, self.x + d, self.core))

    def x_arrived(self, way, step):
        d = 1 if way == 0 else SIDE - 1
        ref = self.w_rows(self.y, self.x + (step + 1) * (SIDE - d), None if step == 0 else way)
        self.z_take(ref, self.xr.at[way, step])

    def y_copy(self, way, step, dx):
        d = 1 if way == 0 else SIDE - 1
        ref = self.w_rows(self.y + step * (SIDE - d), self.x + dx, None if step == 0 else way)
        return self.w_copy(
            self.ws, self.yr.at[way, step, dx], ref, seq_at(self.y + d, self.x, self.core)
        )

    def y_arrived(self, way, step, dx):
        d = 1 if way == 0 else SIDE - 1
        ref = self.w_rows(self.y + (step + 1) * (SIDE - d), self.x + dx, None if step == 0 else way)
        self.z_take(ref, self.yr.at[way, step, dx])

    def c_copy(self, dy, dx):
        ref = self.w_rows(self.y + dy, self.x + dx, None)
        return self.w_copy(
            self.ws, self.cr, ref, seq_at(self.y, self.x, 1 - self.core)
        )

    def s_copy(self, way, chunk, ref):
        into = (self.left if way == 0 else self.right).at[chunk]
        to = (self.seq + (1 if way == 0 else 31)) % 32
        return pltpu.make_async_remote_copy(
            ref, into, self.ss, self.sr.at[way, chunk],
            device_id={"seq": to}, device_id_type=MESH,
        )

    def w_begin(self):
        for way in (0, 1):
            self.x_copy(way, 0).start()
            self.y_copy(way, 0, 0).start()
        self.c_copy(0, 0).start()

    def w_row(self):
        for way, dx in ((0, SIDE - 1), (1, 1)):
            self.x_arrived(way, 0)
            self.x_copy(way, 1).start()
            for to in (0, 1):
                self.y_copy(to, 0, dx).start()
            self.c_copy(0, dx).start()

    def w_far(self):
        for way in (0, 1):
            self.x_arrived(way, 1)
        for to in (0, 1):
            self.y_copy(to, 0, 2).start()
        self.c_copy(0, 2).start()

    def w_near(self, dx):
        for way, dy in ((0, SIDE - 1), (1, 1)):
            self.y_arrived(way, 0, dx)
            self.y_copy(way, 1, dx).start()
            self.c_copy(dy, dx).start()

    def w_last(self, dx):
        for way in (0, 1):
            self.y_arrived(way, 1, dx)
        self.c_copy(2, dx).start()

    def w_end(self):
        self.z_take(self.weight.at[0 : SIDE * SIDE * ROWS_W], self.cr)

    def leave(self):
        for way in (0, 1):
            ref = self.held.at[0 : N_MP // 2 - 1]
            self.z_take(ref, self.zs.at[way, 0])
            self.z_take(self.held.at[0, 0], self.zs.at[way, 1])
        sent = (2 + 2 * SIDE) * (ROWS_W + ROWS_W // 2) + SIDE * SIDE * ROWS_W
        self.z_take(self.weight.at[0:sent], self.ws)
        self.z_take(self.held.at[0, 0], self.ss)


COLS_STEP = 256


def part_product(held, weight, src, half, chunks, cols):
    lhs = jnp.concatenate([held[src, half, q] for q in chunks], axis=1)
    rhs = jnp.concatenate(
        [weight[pl.ds(pl.multiple_of((src * CHUNKS + q) * WIDE, WIDE), WIDE), cols] for q in chunks], axis=0
    )
    return jnp.dot(lhs, rhs, preferred_element_type=F32)


def columns(n):
    return pl.ds(pl.multiple_of(n * COLS_STEP, COLS_STEP), COLS_STEP)


def add_product(held, weight, total, src, half, chunks, fresh=False):
    def body(n, _):
        cols = columns(n)
        value = part_product(held, weight, src, half, chunks, cols)
        if fresh:
            total[half, :, cols] = value
        else:
            total[half, :, cols] += value
        return 0

    lax.fori_loop(0, COLS // COLS_STEP, body, 0)


def finish(held, weight, total, out, src, half, chunks):
    def body(n, _):
        cols = columns(n)
        value = (total[half, :, cols] + part_product(held, weight, src, half, chunks, cols)).astype(BF16)
        if half == 0:
            out[SPILL : SPILL + HALF, cols] = value
        else:
            out[0:SPILL, cols] = value[0:SPILL]
            out[TOK - SPILL : TOK, cols] = value[SPILL:]
        return 0

    lax.fori_loop(0, COLS // COLS_STEP, body, 0)


def finish_rows(held, weight, total, out, src, part, chunks):
    rows = slice(part * SPILL, (part + 1) * SPILL)
    at = part * (TOK - SPILL)

    def body(n, _):
        cols = columns(n)
        lhs = jnp.concatenate([held[src, 1, q, rows] for q in chunks], axis=1)
        rhs = jnp.concatenate(
            [weight[pl.ds(pl.multiple_of((src * CHUNKS + q) * WIDE, WIDE), WIDE), cols] for q in chunks], axis=0
        )
        value = total[1, rows, cols] + jnp.dot(lhs, rhs, preferred_element_type=F32)
        out[at : at + SPILL, cols] = value.astype(BF16)
        return 0

    lax.fori_loop(0, COLS // COLS_STEP, body, 0)


def source_of(mp, u):
    p = u // 2
    far = (p + 1) // 2
    return (mp + N_MP + far * (1 - 2 * (p % 2))) % N_MP


def add_sources(held, weight, total, mp, low, high):
    def body(u, _):
        add_product(held, weight, total, source_of(mp, u), u % 2, range(CHUNKS))
        return 0

    lax.fori_loop(low, high, body, 0)


SEGMENTS = (
    (((2, 6),), ((3, 6),)),
    (((6, 8),), ((6, 8),)),
    (((0, 2), (8, BLOCKS)), ((0, 3), (8, BLOCKS))),
)


def mix_kernel(projections, own_weight, offsets, owners, short_filter, long_filter, skip, out, *scratch):
    panels, masks, later, near, factors, taps, pick, circ, direct, query, product, gated = scratch[:12]
    mine, outgoing, held, weight, total, left, right, in_sem, own_sem = scratch[12:21]
    links = Links(held, weight, left, right, scratch[21:])
    mp = links.mp

    def fetch(q):
        return pltpu.make_async_copy(
            projections.at[:, pl.ds(pl.multiple_of(q * WIDE, WIDE), WIDE), :],
            panels.at[q, :, :, PAD * LONG :],
            in_sem.at[q],
        )

    own = pltpu.make_async_copy(own_weight, links.w_rows(links.y, links.x, None), own_sem)
    links.greet()
    fetch(0).start()
    own.start()
    for q in range(1, CHUNKS):
        fetch(q).start()
    start, coarse, fine, limit = owner_span(links.seq, offsets, owners)
    clear = jnp.zeros((3, WIDE, PAD * LONG), BF16)
    panels[0, :, :, LONG : PAD * LONG] = clear[:, :, LONG:]
    prepare(mp, fine, short_filter, long_filter, near, taps, pick)
    mark_blocks(start, range(2, 6), offsets, masks, later, (2,))
    own.wait()
    fetch(0).wait()

    def spill(way, q):
        return links.s_copy(way, q, outgoing.at[q, way])

    def edges(q):
        for way in (0, 1):
            into = (left if way == 0 else right).at[q]
            links.z_take(into, links.sr.at[way, q])
        held[mp, 1, q, 0:SPILL] = mine[q, 0] + left[q]
        held[mp, 1, q, SPILL : 2 * SPILL] = mine[q, 1] + right[q]
        links.z_begin(q, 2)

    def stages(q, segment, between=None):
        short_ranges, long_ranges = SEGMENTS[segment]
        short_stage(
            mp, q, short_ranges, segment == 0, coarse, panels, near, factors, skip, later, taps, circ, direct, query, product
        )
        if between is not None:
            between()
        for low, high in long_ranges:
            long_stage(q, low, high, masks, circ, direct, query, product, gated)

    def second(piece):
        for way in (0, 1):
            links.relay(way, 2, (piece,))

    def at_chunk(q, steps):
        for n, step in steps:
            pl.when(q == n)(step)

    def opening(q, between=None):
        stages(q, 0, between)
        held[mp, 0, q, 0:SPILL] = place(limit, q, 2, pick, gated)

    opening(0)
    links.meet()
    links.z_begin(0, 0)
    links.w_begin()
    panels[0, :, :, 0:LONG] = clear[:, :, 0:LONG]
    product[:, :, 0:LONG] = jnp.zeros((CHUNKS, WIDE, LONG), BF16)
    gated[:, :, 0:LONG] = jnp.zeros((CHUNKS, WIDE, LONG), BF16)
    mark_blocks(start, (6, 7), offsets, masks, later)

    def middle(q, _):
        stages(q, 1)
        held[mp, 0, q, SPILL : 2 * SPILL] = place(limit, q, 3, pick, gated)
        links.z_begin(q, 1)

        @pl.when(q < CHUNKS - 1)
        def _():
            panels[q + 1, :, :, 0 : PAD * LONG] = clear
            fetch(q + 1).wait()
            opening(q + 1, lambda: pl.when(q == 0)(lambda: links.z_half(0)))
            links.z_begin(q + 1, 0)

        at_chunk(
            q,
            (
                (0, lambda: links.z_half(1)),
                (1, links.w_row),
                (2, lambda: links.z_first(1, 0)),
                (3, lambda: links.z_first(2, 0)),
                (3, links.w_far),
                (3, lambda: links.w_near(0)),
            ),
        )
        return 0

    lax.fori_loop(0, CHUNKS, middle, 0)
    mark_blocks(start, (0, 1, 2, 8, 9, 10, 11), offsets, masks, later)

    def outer(q, _):
        stages(q, 2)
        outgoing[q, 0] = place(limit, q, 5, pick, gated)
        outgoing[q, 1] = place(limit, q, 0, pick, gated)
        for way in (0, 1):
            spill(way, q).start()
        mine[q, 0] = place(limit, q, 1, pick, gated)
        mine[q, 1] = place(limit, q, 4, pick, gated)
        @pl.when(q >= 1)
        def _():
            edges(q - 1)

        at_chunk(
            q,
            (
                (0, lambda: second(0)),
                (1, lambda: links.z_first(3, 0)),
                (2, lambda: second(2)),
                (3, lambda: links.z_first(0, 1)),
                (0, lambda: links.w_near(SIDE - 1)),
                (1, lambda: links.w_near(1)),
                (2, lambda: links.w_near(2)),
            ),
        )
        return 0

    lax.fori_loop(0, CHUNKS, outer, 0)
    edges(CHUNKS - 1)
    links.w_last(0)
    links.w_last(SIDE - 1)
    links.z_first(1, 1)
    links.w_last(1)
    links.w_last(2)
    links.w_end()
    for half in (0, 1):
        add_product(held, weight, total, mp, half, range(CHUNKS), True)
    links.z_first(2, 1)
    links.z_first(3, 1)
    second(4)
    second(6)
    add_sources(held, weight, total, mp, 2, 4)
    second(1)
    add_sources(held, weight, total, mp, 4, 6)
    for k in (3, 5, 7):
        second(k)
    add_sources(held, weight, total, mp, 6, 10)
    for half in (0, 1):
        for k in (0, 1):
            (links.relay_last(0, 3) if (k, half) == (1, 1) else links.relay(0, 3, (2 * k + half,)))
            links.z_arrived(1, 2, 2 * k + half)
        for k in (2, 3):
            (links.relay_last(1, 7) if (k, half) == (3, 1) else links.relay(1, 3, (2 * k + half,)))
            links.z_arrived(0, 2, 2 * k + half)
        for d in (3, N_MP - 3):
            add_product(held, weight, total, (mp + d) % N_MP, half, range(CHUNKS))
    far = (mp + N_MP // 2) % N_MP

    def last(half, k):
        links.z_arrived(0, 3, 2 * k + half)
        links.z_arrived(1, 3, 2 * (k + 2) + half)

    last(0, 0)
    last(0, 1)
    finish(held, weight, total, out, far, 0, range(CHUNKS))
    last(1, 0)
    add_product(held, weight, total, far, 1, (0, 2))
    for part in (0, 1):
        links.last_arrived(0, 3, part)
        links.last_arrived(1, 7, part)
        finish_rows(held, weight, total, out, far, part, (1, 3))
    links.leave()


FILTER_SCRATCH = [
    pltpu.VMEM((CHUNKS, 3, WIDE, PAD * LONG + CAP), BF16),
    pltpu.VMEM((BLOCKS, 2 * LONG, LONG), BF16),
    pltpu.VMEM((SHORT - 1, 8, CAP), F32),
    pltpu.VMEM((3, WIDE, WIDE), F32),
    pltpu.VMEM((CHUNKS, 3 * SHORT, GROUPS, WIDE), F32),
    pltpu.VMEM((CHUNKS * GROUPS, LONG), F32),
    pltpu.VMEM((SPILL, 3 * LONG), BF16),
    pltpu.VMEM((CHUNKS, GROUPS, LONG, LONG), BF16),
    pltpu.VMEM((CHUNKS, WIDE, WIDE), F32),
    pltpu.VMEM((CHUNKS, WIDE, CAP), BF16),
    pltpu.VMEM((CHUNKS, WIDE, LONG + CAP), BF16),
    pltpu.VMEM((CHUNKS, WIDE, LONG + CAP), BF16),
    pltpu.VMEM((CHUNKS, 2, SPILL, WIDE), BF16),
    pltpu.VMEM((CHUNKS, 2, SPILL, WIDE), BF16),
]
LINK_SCRATCH = [
    pltpu.VMEM((N_MP, 2, CHUNKS, HALF, WIDE), BF16),
    pltpu.VMEM((N_MP * DEPTH, COLS), BF16),
    pltpu.VMEM((2, HALF, COLS), F32),
    pltpu.VMEM((CHUNKS, SPILL, WIDE), BF16),
    pltpu.VMEM((CHUNKS, SPILL, WIDE), BF16),
    pltpu.SemaphoreType.DMA((CHUNKS,)),
    pltpu.SemaphoreType.DMA,
    pltpu.SemaphoreType.DMA((2, 2)),
    pltpu.SemaphoreType.DMA((2, CHUNKS, 3)),
    pltpu.SemaphoreType.DMA((2, 3, PIECES)),
    pltpu.SemaphoreType.DMA,
    pltpu.SemaphoreType.DMA((2, 2)),
    pltpu.SemaphoreType.DMA((2, 2, SIDE)),
    pltpu.SemaphoreType.DMA,
    pltpu.SemaphoreType.DMA,
    pltpu.SemaphoreType.DMA((2, CHUNKS)),
]


def per_device(projections, lengths, owners, offsets, short_filter, long_filter, skip, out_weight):
    vmem = pl.BlockSpec(memory_space=pltpu.VMEM)
    anywhere = pl.BlockSpec(memory_space=pl.ANY)
    return pl.pallas_call(
        mix_kernel,
        out_shape=pltpu.VMEM((TOK, COLS), BF16),
        in_specs=[anywhere, anywhere] + [vmem] * 5,
        out_specs=vmem,
        scratch_shapes=FILTER_SCRATCH + LINK_SCRATCH,
        compiler_params=pltpu.CompilerParams(
            collective_id=0, has_side_effects=True, vmem_limit_bytes=60 * 2**20
        ),
    )(
        projections,
        out_weight,
        offsets.reshape(1, -1),
        owners.reshape(1, -1),
        short_filter.transpose(0, 2, 1),
        long_filter,
        skip.reshape(-1, WIDE),
    )


def solution(mesh):
    placed = (P(None, "mp", "seq"), P(), P(), P(), P(), P(), P(), P("seq", "mp"))
    return jax.shard_map(
        per_device, mesh=mesh, in_specs=placed, out_specs=P("seq", "mp"), check_vma=False
    )
```
